128 devices in a mesh: row: 8 (over z, core), col: 16 (over x, y).
Axes of the slice: x: 4, y: 4, z: 4, core: 2. Of those that a mesh axis runs over, the one named last changes fastest.
Arguments:
- far_field: float32 [16384, 16384], P('row', 'col'), may hold values from -4 to 4, as said below
- inverses: float32 [2, 256, 256], replicated, may hold values from -0.05 to 0.06, as said below
- test_table: float32 [524288, 128], P(('row', 'col')), may hold values from -1.5 to 1.5
- trial_table: float32 [524288, 128], P(('row', 'col')), may hold values from -1.5 to 1.5
- tile_list: int32 [2048, 2], P(('row', 'col')), may hold values from 0 to 127, as said below
- tile_nodes: int32 [2048, 256], P(('row', 'col')), may hold values from 0 to 4095
- strokes: float32 [16384, 256], P('col'), may hold values from -0.046875 to 0.046875
Outputs:
- factored: float32 [16384, 16384], P('row', 'col')
- stroke_image: float32 [16384, 256], P('row')
The draws below stay inside these ranges and needn't reach their ends.
Inputs may be any that keep to these rules, and one draw needn't show every extreme that they name: `tile_list`: tile t lies in the block rows held by the grid row of its pair owner (owners in row-major order of the device grid). At most 2 tiles of one owner fall in the block columns of one grid column, and in every grid row some grid column receives exactly 2 tiles from every owner of that row. Duplicate blocks may occur. `tile_nodes`: node indices refer to the owner's own 4096 table rows. `far_field`: entries of order one with a dominant diagonal between 2 and 4. `inverses`: each inverse has a positive diagonal and full off-diagonal entries.
All inputs are finite; a program needn't handle non-finite values.
Results may differ from the reference program's by a relative error of at most 0.0001.
Values sent between devices are 32-bit elements; how exact they have to be, the bound alone decides.
A program may use at most 128 MiB of HBM per device.

```python
import jax
import jax.numpy as jnp
from jax import lax

M = 16384
TILE = 128
W = 256
S = 256
Q = 256
NODES_DEV = 4096
TPD = 16
CAP = 2
N_ROW = 8
N_COL = 16


def draw_far_field(key, part):
    first = jax.random.fold_in(jax.random.fold_in(key, 11), 0)
    third = jax.random.fold_in(jax.random.fold_in(key, 11), 2)
    offdiag = jnp.clip(0.5 * jax.random.normal(first, (M, M), jnp.float32), -1.9, 1.9)
    diagonal = jax.random.uniform(third, (M,), jnp.float32, 2.0, 4.0)
    return offdiag * (1.0 - jnp.eye(M, dtype=jnp.float32)) + jnp.diag(diagonal)


def draw_inverses(key, part):
    first, second = jax.random.split(jax.random.fold_in(key, 23), 2)
    offdiag = jnp.clip(0.004 * jax.random.normal(first, (2, W, W), jnp.float32), -0.02, 0.02)
    diagonal = jax.random.uniform(second, (2, W), jnp.float32, 0.02, 0.06)
    eye = jnp.eye(W, dtype=jnp.float32)
    return offdiag * (1.0 - eye)[None] + diagonal[:, :, None] * eye[None]


def draw_tile_list(key, part):
    base = jax.random.fold_in(key, 37)
    block_rows = M // N_ROW // TILE
    block_cols = M // N_COL // TILE
    slots = N_COL * CAP
    hot = jax.random.randint(jax.random.fold_in(base, 1), (N_ROW,), 0, N_COL)

    def one_owner(owner):
        owner_key = jax.random.fold_in(base, owner + 100)
        first, second, third, fourth = jax.random.split(owner_key, 4)
        grid_row = owner // N_COL
        order = jax.random.permutation(first, slots)
        ranking = jnp.argsort(order).astype(jnp.int32)
        slot_ids = jnp.arange(slots, dtype=jnp.int32)
        is_hot = slot_ids // CAP == hot[grid_row]
        score = jnp.where(is_hot, slot_ids % CAP, ranking + CAP)
        chosen = jnp.argsort(score)[:TPD].astype(jnp.int32)
        chosen = chosen[jax.random.permutation(second, TPD)]
        target = chosen // CAP
        block_row = grid_row * block_rows + jax.random.randint(third, (TPD,), 0, block_rows)
        block_col = target * block_cols + jax.random.randint(fourth, (TPD,), 0, block_cols)
        return jnp.stack([block_row, block_col], axis=1).astype(jnp.int32)
    owners = jnp.arange(N_ROW * N_COL, dtype=jnp.int32)
    return jax.vmap(one_owner)(owners).reshape(N_ROW * N_COL * TPD, 2)


def with_ends(drawn, own_key, low, high):
    spot = [jax.random.randint(jax.random.fold_in(own_key, axis), (), 0, length) for axis, length in enumerate(drawn.shape)]
    widest = drawn.shape.index(max(drawn.shape))
    beside = spot[:widest] + [(spot[widest] + 1) % drawn.shape[widest]] + spot[widest + 1:]
    return drawn.at[tuple(spot)].set(low).at[tuple(beside)].set(high)


def level_of(key, shape, cuts, low, top_value):
    level = 1.0
    for axis_at, blocks in cuts:
        heights = jax.random.uniform(jax.random.fold_in(jax.random.fold_in(key, 6), axis_at), (blocks,), jnp.float32, low / len(cuts), top_value / len(cuts))
        level = level * jnp.repeat(jnp.exp(heights), shape[axis_at] // blocks).reshape((-1,) + (1,) * (len(shape) - 1 - axis_at))
    return level


def centred(own_key, extent, scale, most, pieces=(), kind=jnp.bfloat16):
    gain = level_of(own_key, extent, pieces, -0.22, 0.18) if pieces else 1.0
    array = jax.random.normal(own_key, extent, jnp.float32) * scale * gain
    return jnp.minimum(jnp.maximum(array, -most), most).astype(kind)


def setup_inputs(seed: int = 0) -> dict:
    keys = jax.random.split(jax.random.key(seed), 8)
    far_field = draw_far_field(jax.random.fold_in(keys[7], 71), 0)
    inverses = draw_inverses(jax.random.fold_in(keys[7], 71), 0)
    test_table = centred(keys[2], (N_ROW * N_COL * NODES_DEV, TILE), 0.25, 1.5, ((0, 128),), jnp.float32)
    trial_table = centred(keys[3], (N_ROW * N_COL * NODES_DEV, TILE), 0.25, 1.5, ((0, 128),), jnp.float32)
    tile_list = draw_tile_list(jax.random.fold_in(keys[7], 71), 0)
    tile_nodes = with_ends(jax.random.randint(keys[5], (N_ROW * N_COL * TPD, Q), 0, NODES_DEV), jax.random.fold_in(keys[5], 1), 0, NODES_DEV - 1).astype(jnp.int32)
    strokes = centred(keys[6], (M, S), M ** -0.5, 0.046875, ((0, 16),), jnp.float32)
    return dict(far_field=far_field, inverses=inverses, test_table=test_table, trial_table=trial_table, tile_list=tile_list, tile_nodes=tile_nodes, strokes=strokes)


def reference(far_field, inverses, test_table, trial_table, tile_list, tile_nodes, strokes):
    highest = lax.Precision.HIGHEST

    def add_tile(index, matrix):
        index = jnp.asarray(index).astype(jnp.int32)
        owner = index // TPD
        rows = (owner * NODES_DEV + tile_nodes[index]).astype(jnp.int32)
        left = test_table[rows]
        right = trial_table[rows]
        piece = jnp.dot(left.T, right, precision=highest, preferred_element_type=jnp.float32)
        start_row = (tile_list[index, 0] * TILE).astype(jnp.int32)
        start_col = (tile_list[index, 1] * TILE).astype(jnp.int32)
        current = lax.dynamic_slice(matrix, (start_row, start_col), (TILE, TILE))
        return lax.dynamic_update_slice(matrix, current + piece, (start_row, start_col))

    matrix = lax.fori_loop(0, N_ROW * N_COL * TPD, add_tile, far_field)
    for panel in range(2):
        low = panel * W
        high = low + W
        lower = jnp.dot(matrix[high:, low:high], inverses[panel], precision=highest, preferred_element_type=jnp.float32)
        update = jnp.dot(lower, matrix[low:high, high:], precision=highest, preferred_element_type=jnp.float32)
        matrix = matrix.at[high:, high:].set(matrix[high:, high:] - update)
        matrix = matrix.at[high:, low:high].set(lower)
    image = jnp.dot(matrix, strokes, precision=highest, preferred_element_type=jnp.float32)
    return matrix, image
```

```python
import functools

import jax
import jax.numpy as jnp
from jax import lax
from jax.experimental import pallas as pl
from jax.experimental.pallas import tpu as pltpu
from jax.sharding import PartitionSpec as P

MESH = pl.DeviceIdType.MESH
HIGH = lax.Precision.HIGH
F32 = jnp.float32
VMEM = pltpu.VMEM
DMA = pltpu.SemaphoreType.DMA

LINK_TREE = (
    (0, 1, 2, 3), (1, 1, 1, 4), (3, 1, 1, 3), (3, 4, 3, 3),
    (0, 0, 4, 0), (1, 1, 0, 1), (3, 1, 0, 3), (0, 3, 0, 0),
    (0, 0, 2, 2), (0, 0, 2, 1), (0, 1, 2, 3), (0, 3, 2, 2),
    (4, 2, 2, 2), (2, 2, 2, 1), (2, 1, 1, 3), (2, 3, 3, 3),
)
TREE_DEPTH = (
    (0, 3, 4, 3, 1, 2, 3, 2, 2, 3, 4, 3, 3, 4, 5, 4),
    (0, 1, 2, 3, 3, 2, 3, 4, 4, 3, 4, 5, 3, 2, 3, 4),
    (0, 3, 4, 3, 3, 4, 5, 4, 2, 3, 4, 3, 1, 2, 3, 2),
    (0, 3, 2, 1, 3, 4, 3, 2, 4, 5, 4, 3, 3, 4, 3, 2),
)
STEPS_X = (1, 0, 3, 0)
STEPS_Y = (0, 1, 0, 3)


def table(values, index):
    found = jnp.int32(0)
    for at, value in enumerate(values):
        if value:
            found = found + jnp.where(index == at, jnp.int32(value), jnp.int32(0))
    return found


def mod4(value):
    return lax.rem(value, 4)


def dot(a, b):
    return jnp.dot(a, b, precision=HIGH, preferred_element_type=F32)


def pieces_kernel(tiles_ref, nodes_ref, test_ref, trial_ref, out_ref, left, right, count, label):
    owned, quad = nodes_ref.shape
    dests = out_ref.shape[0]
    tile = test_ref.shape[1]
    block_cols = 8
    block_rows = 16

    def clear(at, carry):
        count[at] = 0
        label[2 * at] = -1
        label[2 * at + 1] = -1
        return carry

    lax.fori_loop(0, dests, clear, 0)

    def one_tile(t, carry):
        for q in range(quad):
            node = nodes_ref[t, q]
            left[pl.ds(q, 1), :] = test_ref[pl.ds(node, 1), :]
            right[pl.ds(q, 1), :] = trial_ref[pl.ds(node, 1), :]
        piece = lax.dot_general(
            left[...], right[...], (((0,), (0,)), ((), ())), precision=HIGH, preferred_element_type=F32
        )
        block_row = lax.rem(tiles_ref[t, 0], block_rows)
        block_col = tiles_ref[t, 1]
        dest = lax.div(block_col, block_cols)
        slot = count[dest]
        count[dest] = slot + 1
        label[2 * dest + slot] = block_row * block_cols + lax.rem(block_col, block_cols)
        out_ref[dest, pl.ds(pl.multiple_of(slot * tile, tile), tile), :] = piece
        return carry

    lax.fori_loop(0, owned, one_tile, 0)
    sublane = lax.broadcasted_iota(jnp.int32, (8, tile), 0)
    for d in range(dests):
        both = jnp.where(sublane == 0, label[2 * d], label[2 * d + 1])
        out_ref[d, 2 * tile : 2 * tile + 8, :] = both.astype(F32)


def make_pieces(tile_list, tile_nodes, test_table, trial_table, dests):
    tile = test_table.shape[1]
    quad = tile_nodes.shape[1]
    return pl.pallas_call(
        pieces_kernel,
        out_shape=jax.ShapeDtypeStruct((dests, 2 * tile + 8, tile), F32),
        in_specs=[
            pl.BlockSpec(memory_space=pltpu.SMEM),
            pl.BlockSpec(memory_space=pltpu.SMEM),
            pl.BlockSpec(memory_space=VMEM),
            pl.BlockSpec(memory_space=VMEM),
        ],
        out_specs=pl.BlockSpec(memory_space=VMEM),
        scratch_shapes=[
            VMEM((quad, tile), F32),
            VMEM((quad, tile), F32),
            pltpu.SMEM((dests,), jnp.int32),
            pltpu.SMEM((2 * dests,), jnp.int32),
        ],
        name="pieces",
    )(tile_list, tile_nodes, test_table, trial_table)


OFFSETS = sorted(
    ((dx, dy) for dx in range(4) for dy in range(4) if dx or dy),
    key=lambda o: -(min(o[0], 4 - o[0]) + min(o[1], 4 - o[1])),
)


def exchange_kernel(packed, arrived, send_sem, recv_sem, own_sem):
    row = lax.axis_index("row")
    col = lax.axis_index("col")
    x, y = lax.div(col, 4), lax.rem(col, 4)
    peers = [mod4(x + dx) * 4 + mod4(y + dy) for dx, dy in OFFSETS]
    barrier = pltpu.get_barrier_semaphore()
    for peer in peers:
        pl.semaphore_signal(barrier, inc=1, device_id=(row, peer), device_id_type=MESH)
    pl.semaphore_wait(barrier, len(peers))
    own = pltpu.make_async_copy(packed.at[col], arrived.at[col], own_sem)
    copies = []
    for k, peer in enumerate(peers):
        copies.append(
            pltpu.make_async_remote_copy(
                src_ref=packed.at[peer],
                dst_ref=arrived.at[col],
                send_sem=send_sem.at[k],
                recv_sem=recv_sem.at[k],
                device_id=(row, peer),
                device_id_type=MESH,
            )
        )
        copies[-1].start()
    own.start()
    own.wait()
    for copy in copies:
        copy.wait()


def exchange(packed):
    n = len(OFFSETS)
    return pl.pallas_call(
        exchange_kernel,
        out_shape=jax.ShapeDtypeStruct(packed.shape, F32),
        in_specs=[pl.BlockSpec(memory_space=VMEM)],
        out_specs=pl.BlockSpec(memory_space=pl.ANY),
        scratch_shapes=[DMA((n,)), DMA((n,)), DMA],
        compiler_params=pltpu.CompilerParams(collective_id=0, has_side_effects=True),
        name="exchange",
    )(packed)


def place_kernel(label_ref, far, arrived, out, block, tiles, in_sem, out_sem, tile_sem):
    rows, cols = block.shape
    chunks = 8
    size = rows // chunks
    tile = tiles.shape[2]
    bring = pltpu.make_async_copy(arrived, tiles, tile_sem)
    bring.start()

    def part(j):
        return pl.ds(j * size, size)

    ins = [pltpu.make_async_copy(far.at[part(j)], block.at[part(j)], in_sem.at[j]) for j in range(chunks)]
    outs = [pltpu.make_async_copy(block.at[part(j)], out.at[part(j)], out_sem.at[j]) for j in range(chunks)]
    for copy in ins:
        copy.start()
    bring.wait()
    for j in range(chunks):
        ins[j].wait()

        def add(s, carry):
            lab = label_ref[s]

            @pl.when((lab >= 0) & (lax.div(lab, 16) == j))
            def _():
                at = (
                    pl.ds(pl.multiple_of(lax.div(lab, 8) * tile, tile), tile),
                    pl.ds(pl.multiple_of(lax.rem(lab, 8) * tile, tile), tile),
                )
                piece = tiles[lax.div(s, 2), pl.ds(pl.multiple_of(lax.rem(s, 2) * tile, tile), tile), :]
                block[at] = block[at] + piece

            return carry

        lax.fori_loop(0, label_ref.shape[0], add, 0)
        outs[j].start()
    for copy in outs:
        copy.wait()


def place(labels, far, arrived):
    return pl.pallas_call(
        place_kernel,
        out_shape=jax.ShapeDtypeStruct(far.shape, F32),
        in_specs=[
            pl.BlockSpec(memory_space=pltpu.SMEM),
            pl.BlockSpec(memory_space=pl.ANY),
            pl.BlockSpec(memory_space=pl.ANY),
        ],
        out_specs=pl.BlockSpec(memory_space=pl.ANY),
        scratch_shapes=[VMEM(far.shape, F32), VMEM(arrived.shape, F32), DMA((8,)), DMA((8,)), DMA],
        name="place",
    )(labels, far, arrived)


P_CHUNKS = 32
P_ROWS = 64
Q_CHUNKS = 16
Q_ROWS = 32
C_CHUNKS = 8


def bcast_kernel(
    asm, p_ref, q_ref, c_ref, load_p, load_q, send_p, recv_p, send_q, recv_q, send_c, recv_c
):
    row = lax.axis_index("row")
    col = lax.axis_index("col")
    x, y = lax.div(col, 4), lax.rem(col, 4)
    z, core = lax.div(row, 2), lax.rem(row, 2)
    source = col == 0
    top = row == 0
    z_up = mod4(z + 1) * 2 + core
    z_down = mod4(z + 3) * 2 + core
    other = z * 2 + 1 - core
    neighbours = [mod4(x + STEPS_X[d]) * 4 + mod4(y + STEPS_Y[d]) for d in range(4)]
    link_tree = [table([LINK_TREE[v][d] for v in range(16)], col) for d in range(4)]
    depth = [table(TREE_DEPTH[t], col) for t in range(4)]

    barrier = pltpu.get_barrier_semaphore()
    for d in range(4):
        pl.semaphore_signal(barrier, inc=1, device_id=(row, neighbours[d]), device_id_type=MESH)
    for r in (z_up, z_down, other):
        pl.semaphore_signal(barrier, inc=1, device_id=(r, col), device_id_type=MESH)

    quarter = p_ref.shape[0] // 4

    def load_quarter(k):
        rows = pl.ds(pl.multiple_of(k * quarter, quarter), quarter)
        return pltpu.make_async_copy(asm.at[rows, pl.ds(0, 512)], p_ref.at[rows, :], load_p.at[k])

    load_rows = pltpu.make_async_copy(asm.at[pl.ds(0, 512), :], q_ref, load_q)

    @pl.when(source)
    def _():
        for k in range(4):
            load_quarter(k).start()

    @pl.when(top)
    def _():
        load_rows.start()

    pl.semaphore_wait(barrier, 7)

    @pl.when(top)
    def _():
        load_rows.wait()

    def p_copy(t, i, d):
        at = p_ref.at[
            pl.ds(pl.multiple_of(i * P_ROWS, P_ROWS), P_ROWS), pl.ds(t * 128, 128)
        ]
        return pltpu.make_async_remote_copy(
            src_ref=at,
            dst_ref=at,
            send_sem=send_p.at[d, i],
            recv_sem=recv_p.at[t, i],
            device_id=(row, neighbours[d]),
            device_id_type=MESH,
        )

    def q_copy(h, j, way, r):
        at = q_ref.at[pl.ds(pl.multiple_of(j * Q_ROWS, Q_ROWS), Q_ROWS), pl.ds(h * 512, 512)]
        return pltpu.make_async_remote_copy(
            src_ref=at,
            dst_ref=at,
            send_sem=send_q.at[h, j, way],
            recv_sem=recv_q.at[h, j],
            device_id=(r, col),
            device_id_type=MESH,
        )

    def c_copy(i, way, r, first):
        rows = pl.ds(pl.multiple_of(i * P_ROWS, P_ROWS), P_ROWS)
        here = c_ref.at[rows, :]
        start = pl.multiple_of(jnp.where(i < C_CHUNKS // 2, 256, 0), 256)
        return pltpu.make_async_remote_copy(
            src_ref=p_ref.at[rows, pl.ds(start, 256)] if first else here,
            dst_ref=here,
            send_sem=send_c.at[i, way],
            recv_sem=recv_c.at[i],
            device_id=(r, col),
            device_id_type=MESH,
        )

    lead = core == 0
    q_depth = [z + core, mod4(4 - z) + core]
    q_next = [(z_up, lead & (z < 3)), (z_down, lead & (z != 1))]
    c_depth = 6 + jnp.where(z == 2, 2, jnp.where(z == 0, 0, 1)) + core

    def step(s, carry):
        for t in range(4):
            i = s - depth[t]

            @pl.when((i >= 0) & (i < P_CHUNKS))
            def _(t=t, i=i):
                if t == 0:

                    @pl.when(source & (lax.rem(i, P_CHUNKS // 4) == 0))
                    def _():
                        load_quarter(lax.div(i, P_CHUNKS // 4)).wait()

                @pl.when(jnp.logical_not(source))
                def _():
                    p_copy(t, i, 0).wait_recv()

                for d in range(4):

                    @pl.when(link_tree[d] == t)
                    def _(d=d):
                        p_copy(t, i, d).start()

        for h in range(2):
            j = s - q_depth[h]

            @pl.when((j >= 0) & (j < Q_CHUNKS))
            def _(h=h, j=j):
                @pl.when(jnp.logical_not(top))
                def _():
                    q_copy(h, j, 0, other).wait_recv()

                @pl.when(lead)
                def _():
                    q_copy(h, j, 0, other).start()

                @pl.when(q_next[h][1])
                def _():
                    q_copy(h, j, 1, q_next[h][0]).start()

        i = s - c_depth

        @pl.when((i >= 0) & (i < C_CHUNKS))
        def _():
            @pl.when(top)
            def _():
                c_copy(i, 0, other, True).start()
                c_copy(i, 1, z_up, True).start()
                c_copy(i, 2, z_down, True).start()

            @pl.when(jnp.logical_not(top))
            def _():
                c_copy(i, 0, other, False).wait_recv()

                @pl.when(lead)
                def _():
                    c_copy(i, 0, other, False).start()

                @pl.when(lead & (z == 1))
                def _():
                    c_copy(i, 1, z_up, False).start()

        return carry

    lax.fori_loop(0, P_CHUNKS + 6, step, 0)

    @pl.when(top)
    def _():
        c_ref[0:256, :] = p_ref[0:256, 256:512]
        c_ref[256:512, :] = p_ref[256:512, 0:256]

    def drain_p(i, carry):
        for d in range(4):

            @pl.when(link_tree[d] < 4)
            def _(d=d):
                p_copy(0, i, d).wait_send()

        return carry

    lax.fori_loop(0, P_CHUNKS, drain_p, 0)

    def drain_q(j, carry):
        for h in range(2):

            @pl.when(lead)
            def _(h=h):
                q_copy(h, j, 0, other).wait_send()

            @pl.when(q_next[h][1])
            def _(h=h):
                q_copy(h, j, 1, q_next[h][0]).wait_send()

        return carry

    lax.fori_loop(0, Q_CHUNKS, drain_q, 0)

    def drain_c(i, carry):
        @pl.when(lead)
        def _():
            c_copy(i, 0, other, False).wait_send()

        @pl.when(top | (lead & (z == 1)))
        def _():
            c_copy(i, 1, z_up, False).wait_send()

        @pl.when(top)
        def _():
            c_copy(i, 2, z_down, False).wait_send()

        return carry

    lax.fori_loop(0, C_CHUNKS, drain_c, 0)


def bcast(asm):
    rows, cols = asm.shape
    vmem = pl.BlockSpec(memory_space=VMEM)
    return pl.pallas_call(
        bcast_kernel,
        out_shape=(
            jax.ShapeDtypeStruct((rows, 512), F32),
            jax.ShapeDtypeStruct((512, cols), F32),
            jax.ShapeDtypeStruct((512, 256), F32),
        ),
        in_specs=[pl.BlockSpec(memory_space=pl.ANY)],
        out_specs=(vmem, vmem, vmem),
        scratch_shapes=[
            DMA((4,)),
            DMA,
            DMA((4, P_CHUNKS)),
            DMA((4, P_CHUNKS)),
            DMA((2, Q_CHUNKS, 2)),
            DMA((2, Q_CHUNKS)),
            DMA((C_CHUNKS, 3)),
            DMA((C_CHUNKS,)),
        ],
        compiler_params=pltpu.CompilerParams(collective_id=1, has_side_effects=True),
        name="bcast",
    )(asm)


def update_kernel(asm_ref, p_ref, q_ref, c_ref, inv_ref, s_ref, out_ref, img_ref, u_ref):
    i = pl.program_id(0)
    row = lax.axis_index("row")
    first_col = lax.axis_index("col") == 0

    @pl.when(i == 0)
    def _():
        ratio = dot(c_ref[256:512, :], inv_ref[0])
        u_ref[0:256, :] = q_ref[0:256, :]
        u_ref[256:512, :] = q_ref[256:512, :] - dot(ratio, q_ref[0:256, :])

        @pl.when(first_col)
        def _():
            u_ref[0:256, 0:256] = jnp.zeros((256, 256), F32)
            u_ref[256:512, 0:512] = jnp.zeros((256, 512), F32)

    below0 = (row > 0) | (i > 0)
    below1 = (row > 0) | (i > 1)
    lower0 = jnp.where(below0, dot(p_ref[:, 0:256], inv_ref[0]), 0.0)
    rest = p_ref[:, 256:512] - dot(lower0, c_ref[0:256, :])
    lower1 = jnp.where(below1, dot(rest, inv_ref[1]), 0.0)
    out_ref[...] = asm_ref[...] - dot(jnp.concatenate([lower0, lower1], axis=1), u_ref[...])

    @pl.when(first_col)
    def _():
        out_ref[:, 0:256] = jnp.where(below0, lower0, asm_ref[:, 0:256])
        out_ref[:, 256:512] = jnp.where(below1, lower1, rest)

    img_ref[...] = dot(out_ref[...], s_ref[...])


def update(asm, p, q, c, inverses, strokes):
    rows, cols = asm.shape
    size = 256

    def whole(shape):
        return pl.BlockSpec(shape, lambda i: (0,) * len(shape))

    def tiles(width):
        return pl.BlockSpec((size, width), lambda i: (i, 0))

    return pl.pallas_call(
        update_kernel,
        grid=(rows // size,),
        out_shape=(
            jax.ShapeDtypeStruct((rows, cols), F32),
            jax.ShapeDtypeStruct((rows, strokes.shape[1]), F32),
        ),
        in_specs=[
            tiles(cols),
            tiles(512),
            whole(q.shape),
            whole(c.shape),
            whole(inverses.shape),
            whole(strokes.shape),
        ],
        out_specs=(tiles(cols), tiles(strokes.shape[1])),
        scratch_shapes=[VMEM((512, cols), F32)],
        name="update",
    )(asm, p, q, c, inverses, strokes)


def image_kernel(part, out, stage1, stage2, send_sem, recv_sem):
    row = lax.axis_index("row")
    col = lax.axis_index("col")
    x, y = lax.div(col, 4), lax.rem(col, 4)
    rows = part.shape[0]
    half = rows // 2
    big = half // 4
    small = big // 4
    across = [mod4(x + k) * 4 + y for k in range(4)]
    along = [x * 4 + mod4(y + k) for k in range(4)]

    barrier = pltpu.get_barrier_semaphore()
    for k in range(1, 4):
        pl.semaphore_signal(barrier, inc=1, device_id=(row, across[k]), device_id_type=MESH)
        pl.semaphore_signal(barrier, inc=1, device_id=(row, along[k]), device_id_type=MESH)
    pl.semaphore_wait(barrier, 6)

    outer = (x, y)
    inner = (y, x)
    outer_peers = (across, along)
    inner_peers = (along, across)

    def remote(src, dst, stage, h, k, peer):
        return pltpu.make_async_remote_copy(
            src_ref=src,
            dst_ref=dst,
            send_sem=send_sem.at[stage, h, k - 1],
            recv_sem=recv_sem.at[stage, h, k - 1],
            device_id=(row, peer),
            device_id_type=MESH,
        )

    def rows_at(start, count):
        return pl.ds(pl.multiple_of(start, count), count)

    order = (2, 1, 3)
    first, second, third, fourth = [], [], [], []
    for k in order:
        for h in range(2):
            to = mod4(outer[h] + k)
            copy = remote(
                part.at[rows_at(h * half + to * big, big), :], stage1.at[h, k - 1], 0, h, k, outer_peers[h][k]
            )
            copy.start()
            first.append((h, copy))
    for h in range(2):
        for g, copy in first:
            if g == h:
                copy.wait_recv()
        total = part[rows_at(h * half + outer[h] * big, big), :]
        for k in range(1, 4):
            total = total + stage1[h, k - 1]
        stage1[h, 3] = total
        for k in order:
            to = mod4(inner[h] + k)
            copy = remote(
                stage1.at[h, 3, rows_at(to * small, small), :], stage2.at[h, k - 1], 1, h, k, inner_peers[h][k]
            )
            copy.start()
            second.append((h, copy))
    for h in range(2):
        for g, copy in second:
            if g == h:
                copy.wait_recv()
        total = stage1[h, 3, rows_at(inner[h] * small, small), :]
        for k in range(1, 4):
            total = total + stage2[h, k - 1]
        mine = rows_at(h * half + outer[h] * big + inner[h] * small, small)
        out[mine, :] = total
        for k in order:
            copy = remote(out.at[mine, :], out.at[mine, :], 2, h, k, inner_peers[h][k])
            copy.start()
            third.append((h, copy))
    for h in range(2):
        for g, copy in third:
            if g == h:
                copy.wait_recv()
        mine = rows_at(h * half + outer[h] * big, big)
        for k in order:
            copy = remote(out.at[mine, :], out.at[mine, :], 3, h, k, outer_peers[h][k])
            copy.start()
            fourth.append((h, copy))
    for _, copy in fourth:
        copy.wait_recv()
    for _, copy in first + second + third + fourth:
        copy.wait_send()


def image_sum(part):
    rows, cols = part.shape
    vmem = pl.BlockSpec(memory_space=VMEM)
    return pl.pallas_call(
        image_kernel,
        out_shape=jax.ShapeDtypeStruct(part.shape, F32),
        in_specs=[vmem],
        out_specs=vmem,
        scratch_shapes=[
            VMEM((2, 4, rows // 8, cols), F32),
            VMEM((2, 3, rows // 32, cols), F32),
            DMA((4, 2, 3)),
            DMA((4, 2, 3)),
        ],
        compiler_params=pltpu.CompilerParams(collective_id=2, has_side_effects=True),
        name="image_sum",
    )(part)


def on_device(far_field, inverses, test_table, trial_table, tile_list, tile_nodes, strokes):
    packed = make_pieces(tile_list, tile_nodes, test_table, trial_table, 16)
    arrived = exchange(packed)
    labels = arrived[:, 256:258, 0].astype(jnp.int32).reshape(32)
    asm = place(labels, far_field, arrived)
    p, q, c = bcast(asm)
    factored, part = update(asm, p, q, c, inverses, strokes)
    image = image_sum(part)
    return factored, image


def solution(mesh):
    return jax.shard_map(
        on_device,
        mesh=mesh,
        in_specs=(
            P("row", "col"),
            P(),
            P(("row", "col"), None),
            P(("row", "col"), None),
            P(("row", "col"), None),
            P(("row", "col"), None),
            P("col", None),
        ),
        out_specs=(P("row", "col"), P("row", None)),
        check_vma=False,
    )
```

```python
import jax
import jax.numpy as jnp
from jax import lax
from jax.experimental import pallas as pl
from jax.experimental.pallas import tpu as pltpu
from jax.sharding import PartitionSpec as P

MESH = pl.DeviceIdType.MESH
F32 = jnp.float32
VMEM = pltpu.VMEM
DMA = pltpu.SemaphoreType.DMA

LINK_TREE = (
    (0, 1, 2, 3), (1, 1, 1, 4), (3, 1, 1, 3), (3, 4, 3, 3),
    (0, 0, 4, 0), (1, 1, 0, 1), (3, 1, 0, 3), (0, 3, 0, 0),
    (0, 0, 2, 2), (0, 0, 2, 1), (0, 1, 2, 3), (0, 3, 2, 2),
    (4, 2, 2, 2), (2, 2, 2, 1), (2, 1, 1, 3), (2, 3, 3, 3),
)
TREE_DEPTH = (
    (0, 3, 4, 3, 1, 2, 3, 2, 2, 3, 4, 3, 3, 4, 5, 4),
    (0, 1, 2, 3, 3, 2, 3, 4, 4, 3, 4, 5, 3, 2, 3, 4),
    (0, 3, 4, 3, 3, 4, 5, 4, 2, 3, 4, 3, 1, 2, 3, 2),
    (0, 3, 2, 1, 3, 4, 3, 2, 4, 5, 4, 3, 3, 4, 3, 2),
)
STEPS_X = (1, 0, 3, 0)
STEPS_Y = (0, 1, 0, 3)


def table(values, index):
    found = jnp.int32(0)
    for at, value in enumerate(values):
        if value:
            found = found + jnp.where(index == at, jnp.int32(value), jnp.int32(0))
    return found


def mod4(value):
    return lax.rem(value, 4)


def split(a):
    high = a.astype(jnp.bfloat16)
    return high, (a - high.astype(F32)).astype(jnp.bfloat16)


def dot_split(a, b):
    def one(u, v):
        return jnp.dot(u, v, preferred_element_type=F32)

    return one(a[0], b[0]) + (one(a[0], b[1]) + one(a[1], b[0]))


def dot(a, b):
    return dot_split(split(a), split(b))


def pieces_kernel(tiles_ref, nodes_ref, test_ref, trial_ref, out_ref, left, right, count, label):
    owned, quad = nodes_ref.shape
    dests = out_ref.shape[0]
    tile = test_ref.shape[1]
    block_cols = 8
    block_rows = 16

    def clear(at, carry):
        count[at] = 0
        label[2 * at] = -1
        label[2 * at + 1] = -1
        return carry

    lax.fori_loop(0, dests, clear, 0)

    def one_tile(t, carry):
        for q in range(quad):
            node = nodes_ref[t, q]
            left[pl.ds(q, 1), :] = test_ref[pl.ds(node, 1), :]
            right[pl.ds(q, 1), :] = trial_ref[pl.ds(node, 1), :]
        piece = dot(left[...].T, right[...])
        block_row = lax.rem(tiles_ref[t, 0], block_rows)
        block_col = tiles_ref[t, 1]
        dest = lax.div(block_col, block_cols)
        slot = count[dest]
        count[dest] = slot + 1
        label[2 * dest + slot] = block_row * block_cols + lax.rem(block_col, block_cols)
        out_ref[dest, pl.ds(pl.multiple_of(slot * tile, tile), tile), :] = piece
        return carry

    lax.fori_loop(0, owned, one_tile, 0)
    sublane = lax.broadcasted_iota(jnp.int32, (8, tile), 0)
    for d in range(dests):
        both = jnp.where(sublane == 0, label[2 * d], label[2 * d + 1])
        out_ref[d, 2 * tile : 2 * tile + 8, :] = both.astype(F32)


def make_pieces(tile_list, tile_nodes, test_table, trial_table, dests):
    tile = test_table.shape[1]
    quad = tile_nodes.shape[1]
    return pl.pallas_call(
        pieces_kernel,
        out_shape=jax.ShapeDtypeStruct((dests, 2 * tile + 8, tile), F32),
        in_specs=[
            pl.BlockSpec(memory_space=pltpu.SMEM),
            pl.BlockSpec(memory_space=pltpu.SMEM),
            pl.BlockSpec(memory_space=VMEM),
            pl.BlockSpec(memory_space=VMEM),
        ],
        out_specs=pl.BlockSpec(memory_space=VMEM),
        scratch_shapes=[
            VMEM((quad, tile), F32),
            VMEM((quad, tile), F32),
            pltpu.SMEM((dests,), jnp.int32),
            pltpu.SMEM((2 * dests,), jnp.int32),
        ],
        name="pieces",
    )(tile_list, tile_nodes, test_table, trial_table)


OFFSETS = sorted(
    ((dx, dy) for dx in range(4) for dy in range(4) if dx or dy),
    key=lambda o: -(min(o[0], 4 - o[0]) + min(o[1], 4 - o[1])),
)


def exchange_kernel(packed, arrived, send_sem, recv_sem, own_sem):
    row = lax.axis_index("row")
    col = lax.axis_index("col")
    x, y = lax.div(col, 4), lax.rem(col, 4)
    peers = [mod4(x + dx) * 4 + mod4(y + dy) for dx, dy in OFFSETS]
    barrier = pltpu.get_barrier_semaphore()
    for peer in peers:
        pl.semaphore_signal(barrier, inc=1, device_id=(row, peer), device_id_type=MESH)
    pl.semaphore_wait(barrier, len(peers))
    own = pltpu.make_async_copy(packed.at[col], arrived.at[col], own_sem)
    copies = []
    for k, peer in enumerate(peers):
        copies.append(
            pltpu.make_async_remote_copy(
                src_ref=packed.at[peer],
                dst_ref=arrived.at[col],
                send_sem=send_sem.at[k],
                recv_sem=recv_sem.at[k],
                device_id=(row, peer),
                device_id_type=MESH,
            )
        )
        copies[-1].start()
    own.start()
    own.wait()
    for copy in copies:
        copy.wait()


def exchange(packed):
    n = len(OFFSETS)
    return pl.pallas_call(
        exchange_kernel,
        out_shape=jax.ShapeDtypeStruct(packed.shape, F32),
        in_specs=[pl.BlockSpec(memory_space=VMEM)],
        out_specs=pl.BlockSpec(memory_space=pl.ANY),
        scratch_shapes=[DMA((n,)), DMA((n,)), DMA],
        compiler_params=pltpu.CompilerParams(collective_id=0, has_side_effects=True),
        name="exchange",
    )(packed)


def place_kernel(label_ref, far, arrived, s_ref, out, g_ref, block, tiles, in_sem, out_sem, tile_sem):
    rows, cols = block.shape
    chunks = 8
    size = rows // chunks
    tile = tiles.shape[2]
    bring = pltpu.make_async_copy(arrived, tiles, tile_sem)
    bring.start()

    def part(j):
        return pl.ds(j * size, size)

    ins = [pltpu.make_async_copy(far.at[part(j)], block.at[part(j)], in_sem.at[j]) for j in range(chunks)]
    outs = [pltpu.make_async_copy(block.at[part(j)], out.at[part(j)], out_sem.at[j]) for j in range(chunks)]
    for copy in ins:
        copy.start()
    strokes = split(s_ref[...])
    bring.wait()
    for j in range(chunks):
        ins[j].wait()

        def add(s, carry):
            lab = label_ref[s]

            @pl.when((lab >= 0) & (lax.div(lab, 16) == j))
            def _():
                at = (
                    pl.ds(pl.multiple_of(lax.div(lab, 8) * tile, tile), tile),
                    pl.ds(pl.multiple_of(lax.rem(lab, 8) * tile, tile), tile),
                )
                piece = tiles[lax.div(s, 2), pl.ds(pl.multiple_of(lax.rem(s, 2) * tile, tile), tile), :]
                block[at] = block[at] + piece

            return carry

        lax.fori_loop(0, label_ref.shape[0], add, 0)
        outs[j].start()
        g_ref[part(j), :] = dot_split(split(block[part(j), :]), strokes)
    for copy in outs:
        copy.wait()


def place(labels, far, arrived, strokes):
    rows = far.shape[0]
    return pl.pallas_call(
        place_kernel,
        out_shape=(
            jax.ShapeDtypeStruct(far.shape, F32),
            jax.ShapeDtypeStruct((rows, strokes.shape[1]), F32),
        ),
        in_specs=[
            pl.BlockSpec(memory_space=pltpu.SMEM),
            pl.BlockSpec(memory_space=pl.ANY),
            pl.BlockSpec(memory_space=pl.ANY),
            pl.BlockSpec(memory_space=VMEM),
        ],
        out_specs=(pl.BlockSpec(memory_space=pl.ANY), pl.BlockSpec(memory_space=VMEM)),
        scratch_shapes=[VMEM(far.shape, F32), VMEM(arrived.shape, F32), DMA((8,)), DMA((8,)), DMA],
        name="place",
    )(labels, far, arrived, strokes)


P_CHUNKS = 32
P_ROWS = 64
Q_CHUNKS = 16
Q_ROWS = 32
C_CHUNKS = 8
LAG = 8


def panel_kernel(
    asm, g_ref, inv_ref, s_ref, l_out, u_out, img, p_ref, q_ref, c_ref, l_ref, u_ref, us_ref, part,
    stage1, stage2, load_p, load_q, send_p, recv_p, send_q, recv_q, send_c, recv_c, out_l, out_u,
    send_i, recv_i
):
    row = lax.axis_index("row")
    col = lax.axis_index("col")
    x, y = lax.div(col, 4), lax.rem(col, 4)
    z, core = lax.div(row, 2), lax.rem(row, 2)
    source = col == 0
    top = row == 0
    z_up = mod4(z + 1) * 2 + core
    z_down = mod4(z + 3) * 2 + core
    other = z * 2 + 1 - core
    neighbours = [mod4(x + STEPS_X[d]) * 4 + mod4(y + STEPS_Y[d]) for d in range(4)]
    link_tree = [table([LINK_TREE[v][d] for v in range(16)], col) for d in range(4)]
    depth = [table(TREE_DEPTH[t], col) for t in range(4)]

    across = [mod4(x + k) * 4 + y for k in range(4)]
    along = [x * 4 + mod4(y + k) for k in range(4)]
    barrier = pltpu.get_barrier_semaphore()
    for k in range(1, 4):
        pl.semaphore_signal(barrier, inc=1, device_id=(row, across[k]), device_id_type=MESH)
        pl.semaphore_signal(barrier, inc=1, device_id=(row, along[k]), device_id_type=MESH)
    for r in (z_up, z_down, other):
        pl.semaphore_signal(barrier, inc=1, device_id=(r, col), device_id_type=MESH)

    quarter = p_ref.shape[0] // 4

    def load_quarter(k):
        rows = pl.ds(pl.multiple_of(k * quarter, quarter), quarter)
        return pltpu.make_async_copy(asm.at[rows, pl.ds(0, 512)], p_ref.at[rows, :], load_p.at[k])

    load_rows = pltpu.make_async_copy(asm.at[pl.ds(0, 512), :], q_ref, load_q)

    @pl.when(source)
    def _():
        for k in range(4):
            load_quarter(k).start()

    @pl.when(top)
    def _():
        load_rows.start()

    pl.semaphore_wait(barrier, 9)

    @pl.when(top)
    def _():
        load_rows.wait()

    def p_copy(t, i, d):
        at = p_ref.at[
            pl.ds(pl.multiple_of(i * P_ROWS, P_ROWS), P_ROWS), pl.ds(t * 128, 128)
        ]
        return pltpu.make_async_remote_copy(
            src_ref=at,
            dst_ref=at,
            send_sem=send_p.at[d, i],
            recv_sem=recv_p.at[t, i],
            device_id=(row, neighbours[d]),
            device_id_type=MESH,
        )

    def q_copy(h, j, way, r):
        at = q_ref.at[pl.ds(pl.multiple_of(j * Q_ROWS, Q_ROWS), Q_ROWS), pl.ds(h * 512, 512)]
        return pltpu.make_async_remote_copy(
            src_ref=at,
            dst_ref=at,
            send_sem=send_q.at[h, j, way],
            recv_sem=recv_q.at[h, j],
            device_id=(r, col),
            device_id_type=MESH,
        )

    def c_copy(i, way, r, first):
        rows = pl.ds(pl.multiple_of(i * P_ROWS, P_ROWS), P_ROWS)
        here = c_ref.at[rows, :]
        start = pl.multiple_of(jnp.where(i < C_CHUNKS // 2, 256, 0), 256)
        return pltpu.make_async_remote_copy(
            src_ref=p_ref.at[rows, pl.ds(start, 256)] if first else here,
            dst_ref=here,
            send_sem=send_c.at[i, way],
            recv_sem=recv_c.at[i],
            device_id=(r, col),
            device_id_type=MESH,
        )

    lead = core == 0
    q_depth = [z + core, mod4(4 - z) + core]
    q_next = [(z_up, lead & (z < 3)), (z_down, lead & (z != 1))]
    c_depth = 1 + LAG * (5 + jnp.where(z == 2, 2, jnp.where(z == 0, 0, 1)) + core)

    def step(s, carry):
        for t in range(4):
            i = s - LAG * depth[t]

            @pl.when((i >= 0) & (i < P_CHUNKS))
            def _(t=t, i=i):
                if t == 0:

                    @pl.when(source & (lax.rem(i, P_CHUNKS // 4) == 0))
                    def _():
                        load_quarter(lax.div(i, P_CHUNKS // 4)).wait()

                @pl.when(jnp.logical_not(source))
                def _():
                    p_copy(t, i, 0).wait_recv()

                for d in range(4):

                    @pl.when(link_tree[d] == t)
                    def _(d=d):
                        p_copy(t, i, d).start()

        for h in range(2):
            j = s - LAG * q_depth[h]

            @pl.when((j >= 0) & (j < Q_CHUNKS))
            def _(h=h, j=j):
                @pl.when(jnp.logical_not(top))
                def _():
                    q_copy(h, j, 0, other).wait_recv()

                @pl.when(lead)
                def _():
                    q_copy(h, j, 0, other).start()

                @pl.when(q_next[h][1])
                def _():
                    q_copy(h, j, 1, q_next[h][0]).start()

        i = s - c_depth

        @pl.when((i >= 0) & (i < C_CHUNKS))
        def _():
            @pl.when(top)
            def _():
                c_copy(i, 0, other, True).start()
                c_copy(i, 1, z_up, True).start()
                c_copy(i, 2, z_down, True).start()

            @pl.when(jnp.logical_not(top))
            def _():
                c_copy(i, 0, other, False).wait_recv()

                @pl.when(lead)
                def _():
                    c_copy(i, 0, other, False).start()

                @pl.when(lead & (z == 1))
                def _():
                    c_copy(i, 1, z_up, False).start()

        return carry

    lax.fori_loop(0, max(P_CHUNKS + 5 * LAG, C_CHUNKS + 1 + 8 * LAG), step, 0)

    @pl.when(top)
    def _():
        c_ref[0:256, :] = p_ref[0:256, 256:512]
        c_ref[256:512, :] = p_ref[256:512, 0:256]

    inv0, inv1 = split(inv_ref[0]), split(inv_ref[1])
    upper0 = q_ref[0:256, :]
    ratio = dot_split(split(c_ref[256:512, :]), inv0)
    u_ref[0:256, :] = upper0
    u_ref[256:512, :] = q_ref[256:512, :] - dot(ratio, upper0)

    @pl.when(source)
    def _():
        u_ref[0:256, 0:256] = jnp.zeros((256, 256), F32)
        u_ref[256:512, 0:512] = jnp.zeros((256, 512), F32)

    copy_u = pltpu.make_async_copy(u_ref, u_out, out_u)
    copy_u.start()
    us_ref[...] = dot(u_ref[...], s_ref[...])

    rows = part.shape[0]
    half = rows // 2
    big = half // 4
    small = big // 4
    outer = (x, y)
    inner = (y, x)
    outer_peers = (across, along)
    inner_peers = (along, across)

    def at(start, count):
        return pl.ds(pl.multiple_of(start, count), count)

    def remote(src, dst, stage, h, k, peer):
        return pltpu.make_async_remote_copy(
            src_ref=src,
            dst_ref=dst,
            send_sem=send_i.at[stage, h, k - 1],
            recv_sem=recv_i.at[stage, h, k - 1],
            device_id=(row, peer),
            device_id_type=MESH,
        )

    def first_copy(h, k):
        to = mod4(jnp.where(h == 0, x, y) + k)
        peer = jnp.where(h == 0, to * 4 + y, x * 4 + to)
        return remote(part.at[at(h * half + to * big, big), :], stage1.at[h, k - 1], 0, h, k, peer)

    def l_copy(j):
        return pltpu.make_async_copy(l_ref.at[at(j * big, big), :], l_out.at[at(j * big, big), :], out_l.at[j])

    def one_tile(n, carry):
        h = lax.rem(n, 2)
        k = table((2, 1, 3, 0), lax.div(n, 2))
        j = h * 4 + mod4(jnp.where(h == 0, x, y) + k)
        mine = at(j * big, big)
        below0 = (row > 0) | (j > 0)
        below1 = (row > 0) | (j > 1)
        p0 = p_ref[mine, 0:256]
        lower0 = jnp.where(below0, dot_split(split(p0), inv0), 0.0)
        rest = p_ref[mine, 256:512] - dot(lower0, c_ref[0:256, :])
        lower1 = jnp.where(below1, dot_split(split(rest), inv1), 0.0)
        l_ref[mine, 0:256] = lower0
        l_ref[mine, 256:512] = lower1
        l_copy(j).start()
        part[mine, :] = g_ref[mine, :] - dot(lower0, us_ref[0:256, :]) - dot(lower1, us_ref[256:512, :])

        @pl.when(source)
        def _():
            change0 = jnp.where(below0, lower0 - p0, 0.0)
            change1 = jnp.where(below1, lower1 - rest, 0.0)
            part[mine, :] += dot(change0, s_ref[0:256, :]) + dot(change1, s_ref[256:512, :])

        @pl.when(k > 0)
        def _():
            first_copy(h, k).start()

        return carry

    lax.fori_loop(0, 8, one_tile, 0)

    order = (2, 1, 3)
    second, third, fourth = [], [], []
    for h in range(2):
        for k in order:
            first_copy(h, k).wait_recv()
        total = part[at(h * half + outer[h] * big, big), :]
        for k in range(1, 4):
            total = total + stage1[h, k - 1]
        stage1[h, 3] = total
        for k in order:
            to = mod4(inner[h] + k)
            copy = remote(
                stage1.at[h, 3, at(to * small, small), :], stage2.at[h, k - 1], 1, h, k, inner_peers[h][k]
            )
            copy.start()
            second.append((h, copy))
    for h in range(2):
        for g, copy in second:
            if g == h:
                copy.wait_recv()
        total = stage1[h, 3, at(inner[h] * small, small), :]
        for k in range(1, 4):
            total = total + stage2[h, k - 1]
        mine = at(h * half + outer[h] * big + inner[h] * small, small)
        img[mine, :] = total
        for k in order:
            copy = remote(img.at[mine, :], img.at[mine, :], 2, h, k, inner_peers[h][k])
            copy.start()
            third.append((h, copy))
    for h in range(2):
        for g, copy in third:
            if g == h:
                copy.wait_recv()
        mine = at(h * half + outer[h] * big, big)
        for k in order:
            copy = remote(img.at[mine, :], img.at[mine, :], 3, h, k, outer_peers[h][k])
            copy.start()
            fourth.append((h, copy))
    for _, copy in fourth:
        copy.wait_recv()
    for h in range(2):
        for k in order:
            first_copy(h, k).wait_send()
    for _, copy in second + third + fourth:
        copy.wait_send()
    copy_u.wait()
    for j in range(8):
        l_copy(j).wait()

    def drain_p(i, carry):
        for d in range(4):

            @pl.when(link_tree[d] < 4)
            def _(d=d):
                p_copy(0, i, d).wait_send()

        return carry

    lax.fori_loop(0, P_CHUNKS, drain_p, 0)

    def drain_q(j, carry):
        for h in range(2):

            @pl.when(lead)
            def _(h=h):
                q_copy(h, j, 0, other).wait_send()

            @pl.when(q_next[h][1])
            def _(h=h):
                q_copy(h, j, 1, q_next[h][0]).wait_send()

        return carry

    lax.fori_loop(0, Q_CHUNKS, drain_q, 0)

    def drain_c(i, carry):
        @pl.when(lead)
        def _():
            c_copy(i, 0, other, False).wait_send()

        @pl.when(top | (lead & (z == 1)))
        def _():
            c_copy(i, 1, z_up, False).wait_send()

        @pl.when(top)
        def _():
            c_copy(i, 2, z_down, False).wait_send()

        return carry

    lax.fori_loop(0, C_CHUNKS, drain_c, 0)


def panels(asm, g, inverses, strokes):
    rows, cols = asm.shape
    modes = strokes.shape[1]
    vmem = pl.BlockSpec(memory_space=VMEM)
    hbm = pl.BlockSpec(memory_space=pl.ANY)
    return pl.pallas_call(
        panel_kernel,
        out_shape=(
            jax.ShapeDtypeStruct((rows, 512), F32),
            jax.ShapeDtypeStruct((512, cols), F32),
            jax.ShapeDtypeStruct((rows, modes), F32),
        ),
        in_specs=[hbm, vmem, vmem, vmem],
        out_specs=(hbm, hbm, vmem),
        scratch_shapes=[
            VMEM((rows, 512), F32),
            VMEM((512, cols), F32),
            VMEM((512, 256), F32),
            VMEM((rows, 512), F32),
            VMEM((512, cols), F32),
            VMEM((512, modes), F32),
            VMEM((rows, modes), F32),
            VMEM((2, 4, rows // 8, modes), F32),
            VMEM((2, 3, rows // 32, modes), F32),
            DMA((4,)),
            DMA,
            DMA((4, P_CHUNKS)),
            DMA((4, P_CHUNKS)),
            DMA((2, Q_CHUNKS, 2)),
            DMA((2, Q_CHUNKS)),
            DMA((C_CHUNKS, 3)),
            DMA((C_CHUNKS,)),
            DMA((8,)),
            DMA,
            DMA((4, 2, 3)),
            DMA((4, 2, 3)),
        ],
        compiler_params=pltpu.CompilerParams(collective_id=1, has_side_effects=True),
        name="panels",
    )(asm, g, inverses, strokes)


def update_kernel(asm_ref, l_ref, u_ref, image_ref, out_ref, img_ref, u_high, u_low):
    i = pl.program_id(0)
    row = lax.axis_index("row")

    @pl.when(i == 0)
    def _():
        u_high[...], u_low[...] = split(u_ref[...])

    lower = l_ref[...]
    out_ref[...] = asm_ref[...] - dot_split(split(lower), (u_high[...], u_low[...]))
    img_ref[...] = image_ref[...]

    @pl.when(lax.axis_index("col") == 0)
    def _():
        @pl.when((row > 0) | (i > 0))
        def _():
            out_ref[:, 0:256] = lower[:, 0:256]

        @pl.when((row > 0) | (i > 1))
        def _():
            out_ref[:, 256:512] = lower[:, 256:512]


def update(asm, lower, upper, image):
    rows, cols = asm.shape
    size = 256

    def tiles(width):
        return pl.BlockSpec((size, width), lambda i: (i, 0))

    return pl.pallas_call(
        update_kernel,
        grid=(rows // size,),
        out_shape=(
            jax.ShapeDtypeStruct((rows, cols), F32),
            jax.ShapeDtypeStruct(image.shape, F32),
        ),
        in_specs=[
            tiles(cols),
            tiles(512),
            pl.BlockSpec(upper.shape, lambda i: (0, 0)),
            tiles(image.shape[1]),
        ],
        out_specs=(tiles(cols), tiles(image.shape[1])),
        scratch_shapes=[VMEM(upper.shape, jnp.bfloat16), VMEM(upper.shape, jnp.bfloat16)],
        name="update",
    )(asm, lower, upper, image)


def on_device(far_field, inverses, test_table, trial_table, tile_list, tile_nodes, strokes):
    packed = make_pieces(tile_list, tile_nodes, test_table, trial_table, 16)
    arrived = exchange(packed)
    labels = arrived[:, 256:258, 0].astype(jnp.int32).reshape(32)
    asm, g = place(labels, far_field, arrived, strokes)
    lower, upper, image = panels(asm, g, inverses, strokes)
    return update(asm, lower, upper, image)


def solution(mesh):
    return jax.shard_map(
        on_device,
        mesh=mesh,
        in_specs=(
            P("row", "col"),
            P(),
            P(("row", "col"), None),
            P(("row", "col"), None),
            P(("row", "col"), None),
            P(("row", "col"), None),
            P("col", None),
        ),
        out_specs=(P("row", "col"), P("row", None)),
        check_vma=False,
    )
```

```python
import jax
import jax.numpy as jnp
from jax import lax
from jax.experimental import pallas as pl
from jax.experimental.pallas import tpu as pltpu
from jax.sharding import PartitionSpec as P

MESH = pl.DeviceIdType.MESH
F32 = jnp.float32
VMEM = pltpu.VMEM
DMA = pltpu.SemaphoreType.DMA

LINK_TREE = (
    (0, 1, 2, 3), (1, 1, 1, 4), (3, 1, 1, 3), (3, 4, 3, 3),
    (0, 0, 4, 0), (1, 1, 0, 1), (3, 1, 0, 3), (0, 3, 0, 0),
    (0, 0, 2, 2), (0, 0, 2, 1), (0, 1, 2, 3), (0, 3, 2, 2),
    (4, 2, 2, 2), (2, 2, 2, 1), (2, 1, 1, 3), (2, 3, 3, 3),
)
TREE_DEPTH = (
    (0, 3, 4, 3, 1, 2, 3, 2, 2, 3, 4, 3, 3, 4, 5, 4),
    (0, 1, 2, 3, 3, 2, 3, 4, 4, 3, 4, 5, 3, 2, 3, 4),
    (0, 3, 4, 3, 3, 4, 5, 4, 2, 3, 4, 3, 1, 2, 3, 2),
    (0, 3, 2, 1, 3, 4, 3, 2, 4, 5, 4, 3, 3, 4, 3, 2),
)
STEPS_X = (1, 0, 3, 0)
STEPS_Y = (0, 1, 0, 3)


def table(values, index):
    found = jnp.int32(0)
    for at, value in enumerate(values):
        if value:
            found = found + jnp.where(index == at, jnp.int32(value), jnp.int32(0))
    return found


def mod4(value):
    return lax.rem(value, 4)


def split(a):
    high = a.astype(jnp.bfloat16)
    return high, (a - high.astype(F32)).astype(jnp.bfloat16)


def dot_split(a, b):
    def one(u, v):
        return jnp.dot(u, v, preferred_element_type=F32)

    return one(a[0], b[0]) + (one(a[0], b[1]) + one(a[1], b[0]))


def dot(a, b):
    return dot_split(split(a), split(b))


def pieces_kernel(tiles_ref, nodes_ref, test_ref, trial_ref, out_ref, left, right, count, label):
    owned, quad = nodes_ref.shape
    dests = out_ref.shape[0]
    tile = test_ref.shape[1]
    block_cols = 8
    block_rows = 16

    def clear(at, carry):
        count[at] = 0
        label[2 * at] = -1
        label[2 * at + 1] = -1
        return carry

    lax.fori_loop(0, dests, clear, 0)

    def one_tile(t, carry):
        for q in range(quad):
            node = nodes_ref[t, q]
            left[pl.ds(q, 1), :] = test_ref[pl.ds(node, 1), :]
            right[pl.ds(q, 1), :] = trial_ref[pl.ds(node, 1), :]
        piece = dot(left[...].T, right[...])
        block_row = lax.rem(tiles_ref[t, 0], block_rows)
        block_col = tiles_ref[t, 1]
        dest = lax.div(block_col, block_cols)
        slot = count[dest]
        count[dest] = slot + 1
        label[2 * dest + slot] = block_row * block_cols + lax.rem(block_col, block_cols)
        out_ref[dest, pl.ds(pl.multiple_of(slot * tile, tile), tile), :] = piece
        return carry

    lax.fori_loop(0, owned, one_tile, 0)
    sublane = lax.broadcasted_iota(jnp.int32, (8, tile), 0)
    for d in range(dests):
        both = jnp.where(sublane == 0, label[2 * d], label[2 * d + 1])
        out_ref[d, 2 * tile : 2 * tile + 8, :] = both.astype(F32)


def make_pieces(tile_list, tile_nodes, test_table, trial_table, dests):
    tile = test_table.shape[1]
    quad = tile_nodes.shape[1]
    return pl.pallas_call(
        pieces_kernel,
        out_shape=VMEM((dests, 2 * tile + 8, tile), F32),
        in_specs=[
            pl.BlockSpec(memory_space=pltpu.SMEM),
            pl.BlockSpec(memory_space=pltpu.SMEM),
            pl.BlockSpec(memory_space=VMEM),
            pl.BlockSpec(memory_space=VMEM),
        ],
        out_specs=pl.BlockSpec(memory_space=VMEM),
        scratch_shapes=[
            VMEM((quad, tile), F32),
            VMEM((quad, tile), F32),
            pltpu.SMEM((dests,), jnp.int32),
            pltpu.SMEM((2 * dests,), jnp.int32),
        ],
        compiler_params=pltpu.CompilerParams(vmem_limit_bytes=8 << 20),
        name="pieces",
    )(tile_list, tile_nodes, test_table, trial_table)


OFFSETS = sorted(
    ((dx, dy) for dx in range(4) for dy in range(4) if dx or dy),
    key=lambda o: min(o[0], 4 - o[0]) + min(o[1], 4 - o[1]),
)
FAR_PARTS = 8


def resident(array):
    return pltpu.with_memory_space_constraint(array, VMEM)


def exchange_kernel(packed, far_hbm, s_hbm, arrived, far, g, strokes, send_sem, recv_sem, own_sem, far_sem, s_sem):
    row = lax.axis_index("row")
    col = lax.axis_index("col")
    x, y = lax.div(col, 4), lax.rem(col, 4)
    peers = [mod4(x + dx) * 4 + mod4(y + dy) for dx, dy in OFFSETS]
    barrier = pltpu.get_barrier_semaphore()
    for peer in peers:
        pl.semaphore_signal(barrier, inc=1, device_id=(row, peer), device_id_type=MESH)
    size = far.shape[0] // FAR_PARTS
    load_s = pltpu.make_async_copy(s_hbm, strokes, s_sem)
    load_s.start()
    loads = []
    for j in range(FAR_PARTS):
        part = pl.ds(j * size, size)
        loads.append(pltpu.make_async_copy(far_hbm.at[part], far.at[part], far_sem.at[j]))
        loads[-1].start()
    pl.semaphore_wait(barrier, len(peers))
    copies = []
    for k, peer in enumerate(peers):
        copies.append(
            pltpu.make_async_remote_copy(
                src_ref=packed.at[peer],
                dst_ref=arrived.at[col],
                send_sem=send_sem.at[k],
                recv_sem=recv_sem.at[k],
                device_id=(row, peer),
                device_id_type=MESH,
            )
        )
        copies[-1].start()
    own = pltpu.make_async_copy(packed.at[col], arrived.at[col], own_sem)
    own.start()
    load_s.wait()
    both = split(strokes[...])
    for j in range(FAR_PARTS):
        loads[j].wait()
        part = pl.ds(j * size, size)
        g[part, :] = dot_split(split(far[part, :]), both)
    own.wait()
    for copy in copies:
        copy.wait()


def exchange(packed, far, strokes):
    n = len(OFFSETS)
    hbm = pl.BlockSpec(memory_space=pltpu.HBM)
    vmem = pl.BlockSpec(memory_space=VMEM)
    return pl.pallas_call(
        exchange_kernel,
        out_shape=(
            VMEM(packed.shape, F32),
            VMEM(far.shape, F32),
            VMEM((far.shape[0], strokes.shape[1]), F32),
            VMEM(strokes.shape, F32),
        ),
        in_specs=[vmem, hbm, hbm],
        out_specs=(vmem,) * 4,
        scratch_shapes=[DMA((n,)), DMA((n,)), DMA, DMA((FAR_PARTS,)), DMA],
        compiler_params=pltpu.CompilerParams(
            collective_id=0, has_side_effects=True, vmem_limit_bytes=8 << 20
        ),
        name="exchange",
    )(
        resident(packed),
        pltpu.with_memory_space_constraint(far, pltpu.HBM),
        pltpu.with_memory_space_constraint(strokes, pltpu.HBM),
    )


def place_kernel(arrived, far, g0, strokes, out, g, label):
    tile = arrived.shape[2]
    for d in range(arrived.shape[0]):
        for k in range(2):
            at = 2 * tile + k
            label[2 * d + k] = jnp.max(arrived[d, at : at + 1, :]).astype(jnp.int32)

    def add(s, carry):
        lab = label[s]

        @pl.when(lab >= 0)
        def _():
            rows = pl.ds(pl.multiple_of(lax.div(lab, 8) * tile, tile), tile)
            cols = pl.ds(pl.multiple_of(lax.rem(lab, 8) * tile, tile), tile)
            piece = arrived[lax.div(s, 2), pl.ds(pl.multiple_of(lax.rem(s, 2) * tile, tile), tile), :]
            out[rows, cols] = out[rows, cols] + piece
            g[rows, :] = g[rows, :] + dot(piece, strokes[cols, :])

        return carry

    lax.fori_loop(0, label.shape[0], add, 0)


def place(arrived, far, g, strokes):
    vmem = pl.BlockSpec(memory_space=VMEM)
    return pl.pallas_call(
        place_kernel,
        out_shape=(VMEM(far.shape, F32), VMEM(g.shape, F32)),
        in_specs=[vmem] * 4,
        out_specs=(vmem, vmem),
        scratch_shapes=[pltpu.SMEM((2 * arrived.shape[0],), jnp.int32)],
        input_output_aliases={1: 0, 2: 1},
        compiler_params=pltpu.CompilerParams(vmem_limit_bytes=8 << 20),
        name="place",
    )(resident(arrived), resident(far), resident(g), resident(strokes))


P_CHUNKS = 32
P_ROWS = 64
Q_CHUNKS = 16
Q_ROWS = 32
C_CHUNKS = 8
LAG = 8


def panel_kernel(
    asm, g_ref, inv_ref, s_ref, out_ref, img, p_ref, q_ref, c_ref, l_ref, u_ref, u_high, u_low, us_ref,
    part, stage1, stage2, load_p, load_q, send_p, recv_p, send_q, recv_q, send_c, recv_c, send_i, recv_i
):
    row = lax.axis_index("row")
    col = lax.axis_index("col")
    x, y = lax.div(col, 4), lax.rem(col, 4)
    z, core = lax.div(row, 2), lax.rem(row, 2)
    source = col == 0
    top = row == 0
    z_up = mod4(z + 1) * 2 + core
    z_down = mod4(z + 3) * 2 + core
    other = z * 2 + 1 - core
    neighbours = [mod4(x + STEPS_X[d]) * 4 + mod4(y + STEPS_Y[d]) for d in range(4)]
    link_tree = [table([LINK_TREE[v][d] for v in range(16)], col) for d in range(4)]
    depth = [table(TREE_DEPTH[t], col) for t in range(4)]

    across = [mod4(x + k) * 4 + y for k in range(4)]
    along = [x * 4 + mod4(y + k) for k in range(4)]
    barrier = pltpu.get_barrier_semaphore()
    for k in range(1, 4):
        pl.semaphore_signal(barrier, inc=1, device_id=(row, across[k]), device_id_type=MESH)
        pl.semaphore_signal(barrier, inc=1, device_id=(row, along[k]), device_id_type=MESH)
    for r in (z_up, z_down, other):
        pl.semaphore_signal(barrier, inc=1, device_id=(r, col), device_id_type=MESH)

    quarter = p_ref.shape[0] // 4

    def load_quarter(k):
        rows = pl.ds(pl.multiple_of(k * quarter, quarter), quarter)
        return pltpu.make_async_copy(asm.at[rows, pl.ds(0, 512)], p_ref.at[rows, :], load_p.at[k])

    load_rows = pltpu.make_async_copy(asm.at[pl.ds(0, 512), :], q_ref, load_q)

    @pl.when(source)
    def _():
        for k in range(4):
            load_quarter(k).start()

    @pl.when(top)
    def _():
        load_rows.start()

    pl.semaphore_wait(barrier, 9)

    @pl.when(top)
    def _():
        load_rows.wait()

    def p_copy(t, i, d):
        at = p_ref.at[
            pl.ds(pl.multiple_of(i * P_ROWS, P_ROWS), P_ROWS), pl.ds(t * 128, 128)
        ]
        return pltpu.make_async_remote_copy(
            src_ref=at,
            dst_ref=at,
            send_sem=send_p.at[d, i],
            recv_sem=recv_p.at[t, i],
            device_id=(row, neighbours[d]),
            device_id_type=MESH,
        )

    def q_copy(h, j, way, r):
        at = q_ref.at[pl.ds(pl.multiple_of(j * Q_ROWS, Q_ROWS), Q_ROWS), pl.ds(h * 512, 512)]
        return pltpu.make_async_remote_copy(
            src_ref=at,
            dst_ref=at,
            send_sem=send_q.at[h, j, way],
            recv_sem=recv_q.at[h, j],
            device_id=(r, col),
            device_id_type=MESH,
        )

    def c_copy(i, way, r, first):
        rows = pl.ds(pl.multiple_of(i * P_ROWS, P_ROWS), P_ROWS)
        here = c_ref.at[rows, :]
        start = pl.multiple_of(jnp.where(i < C_CHUNKS // 2, 256, 0), 256)
        return pltpu.make_async_remote_copy(
            src_ref=p_ref.at[rows, pl.ds(start, 256)] if first else here,
            dst_ref=here,
            send_sem=send_c.at[i, way],
            recv_sem=recv_c.at[i],
            device_id=(r, col),
            device_id_type=MESH,
        )

    lead = core == 0
    q_depth = [z + core, mod4(4 - z) + core]
    q_next = [(z_up, lead & (z < 3)), (z_down, lead & (z != 1))]
    c_depth = 1 + LAG * (5 + jnp.where(z == 2, 2, jnp.where(z == 0, 0, 1)) + core)

    def step(s, carry):
        for t in range(4):
            i = s - LAG * depth[t]

            @pl.when((i >= 0) & (i < P_CHUNKS))
            def _(t=t, i=i):
                if t == 0:

                    @pl.when(source & (lax.rem(i, P_CHUNKS // 4) == 0))
                    def _():
                        load_quarter(lax.div(i, P_CHUNKS // 4)).wait()

                @pl.when(jnp.logical_not(source))
                def _():
                    p_copy(t, i, 0).wait_recv()

                for d in range(4):

                    @pl.when(link_tree[d] == t)
                    def _(d=d):
                        p_copy(t, i, d).start()

        for h in range(2):
            j = s - LAG * q_depth[h]

            @pl.when((j >= 0) & (j < Q_CHUNKS))
            def _(h=h, j=j):
                @pl.when(jnp.logical_not(top))
                def _():
                    q_copy(h, j, 0, other).wait_recv()

                @pl.when(lead)
                def _():
                    q_copy(h, j, 0, other).start()

                @pl.when(q_next[h][1])
                def _():
                    q_copy(h, j, 1, q_next[h][0]).start()

        i = s - c_depth

        @pl.when((i >= 0) & (i < C_CHUNKS))
        def _():
            @pl.when(top)
            def _():
                c_copy(i, 0, other, True).start()
                c_copy(i, 1, z_up, True).start()
                c_copy(i, 2, z_down, True).start()

            @pl.when(jnp.logical_not(top))
            def _():
                c_copy(i, 0, other, False).wait_recv()

                @pl.when(lead)
                def _():
                    c_copy(i, 0, other, False).start()

                @pl.when(lead & (z == 1))
                def _():
                    c_copy(i, 1, z_up, False).start()

        return carry

    lax.fori_loop(0, max(P_CHUNKS + 5 * LAG, C_CHUNKS + 1 + 8 * LAG), step, 0)

    @pl.when(top)
    def _():
        c_ref[0:256, :] = p_ref[0:256, 256:512]
        c_ref[256:512, :] = p_ref[256:512, 0:256]

    inv0, inv1 = split(inv_ref[0]), split(inv_ref[1])
    upper0 = q_ref[0:256, :]
    ratio = dot_split(split(c_ref[256:512, :]), inv0)
    u_ref[0:256, :] = upper0
    u_ref[256:512, :] = q_ref[256:512, :] - dot(ratio, upper0)

    @pl.when(source)
    def _():
        u_ref[0:256, 0:256] = jnp.zeros((256, 256), F32)
        u_ref[256:512, 0:512] = jnp.zeros((256, 512), F32)

    u_high[...], u_low[...] = split(u_ref[...])
    us_ref[...] = dot_split((u_high[...], u_low[...]), split(s_ref[...]))

    rows = part.shape[0]
    half = rows // 2
    big = half // 4
    small = big // 4
    outer = (x, y)
    inner = (y, x)
    outer_peers = (across, along)
    inner_peers = (along, across)

    def at(start, count):
        return pl.ds(pl.multiple_of(start, count), count)

    def remote(src, dst, stage, h, k, peer):
        return pltpu.make_async_remote_copy(
            src_ref=src,
            dst_ref=dst,
            send_sem=send_i.at[stage, h, k - 1],
            recv_sem=recv_i.at[stage, h, k - 1],
            device_id=(row, peer),
            device_id_type=MESH,
        )

    def first_copy(h, k):
        to = mod4(jnp.where(h == 0, x, y) + k)
        peer = jnp.where(h == 0, to * 4 + y, x * 4 + to)
        return remote(part.at[at(h * half + to * big, big), :], stage1.at[h, k - 1], 0, h, k, peer)

    def finish_tile(j, carry):
        mine = at(j * big, big)
        lower = l_ref[mine, :]
        out_ref[mine, :] = asm[mine, :] - dot_split(split(lower), (u_high[...], u_low[...]))

        @pl.when(source & ((row > 0) | (j > 0)))
        def _():
            out_ref[mine, 0:256] = l_ref[mine, 0:256]

        @pl.when(source & ((row > 0) | (j > 1)))
        def _():
            out_ref[mine, 256:512] = l_ref[mine, 256:512]

        return carry

    def one_tile(n, carry):
        h = lax.rem(n, 2)
        k = table((2, 1, 3, 0), lax.div(n, 2))
        j = h * 4 + mod4(jnp.where(h == 0, x, y) + k)
        mine = at(j * big, big)
        below0 = (row > 0) | (j > 0)
        below1 = (row > 0) | (j > 1)
        p0 = p_ref[mine, 0:256]
        lower0 = jnp.where(below0, dot_split(split(p0), inv0), 0.0)
        rest = p_ref[mine, 256:512] - dot(lower0, c_ref[0:256, :])
        lower1 = jnp.where(below1, dot_split(split(rest), inv1), 0.0)
        l_ref[mine, 0:256] = lower0
        l_ref[mine, 256:512] = lower1
        part[mine, :] = g_ref[mine, :] - dot(lower0, us_ref[0:256, :]) - dot(lower1, us_ref[256:512, :])

        @pl.when(source)
        def _():
            change0 = jnp.where(below0, lower0 - p0, 0.0)
            change1 = jnp.where(below1, lower1 - rest, 0.0)
            part[mine, :] += dot(change0, s_ref[0:256, :]) + dot(change1, s_ref[256:512, :])

        @pl.when(k > 0)
        def _():
            first_copy(h, k).start()

        return carry

    lax.fori_loop(0, 8, one_tile, 0)

    order = (2, 1, 3)
    second, third, fourth = [], [], []
    for h in range(2):
        for k in order:
            first_copy(h, k).wait_recv()
        total = part[at(h * half + outer[h] * big, big), :]
        for k in range(1, 4):
            total = total + stage1[h, k - 1]
        stage1[h, 3] = total
        for k in order:
            to = mod4(inner[h] + k)
            copy = remote(
                stage1.at[h, 3, at(to * small, small), :], stage2.at[h, k - 1], 1, h, k, inner_peers[h][k]
            )
            copy.start()
            second.append((h, copy))
    lax.fori_loop(0, 2, finish_tile, 0)
    for h in range(2):
        for g, copy in second:
            if g == h:
                copy.wait_recv()
        total = stage1[h, 3, at(inner[h] * small, small), :]
        for k in range(1, 4):
            total = total + stage2[h, k - 1]
        mine = at(h * half + outer[h] * big + inner[h] * small, small)
        img[mine, :] = total
        for k in order:
            copy = remote(img.at[mine, :], img.at[mine, :], 2, h, k, inner_peers[h][k])
            copy.start()
            third.append((h, copy))
    lax.fori_loop(2, 4, finish_tile, 0)
    for h in range(2):
        for g, copy in third:
            if g == h:
                copy.wait_recv()
        mine = at(h * half + outer[h] * big, big)
        for k in order:
            copy = remote(img.at[mine, :], img.at[mine, :], 3, h, k, outer_peers[h][k])
            copy.start()
            fourth.append((h, copy))
    lax.fori_loop(4, 8, finish_tile, 0)
    for _, copy in fourth:
        copy.wait_recv()
    for h in range(2):
        for k in order:
            first_copy(h, k).wait_send()
    for _, copy in second + third + fourth:
        copy.wait_send()
    def drain_p(i, carry):
        for d in range(4):

            @pl.when(link_tree[d] < 4)
            def _(d=d):
                p_copy(0, i, d).wait_send()

        return carry

    lax.fori_loop(0, P_CHUNKS, drain_p, 0)

    def drain_q(j, carry):
        for h in range(2):

            @pl.when(lead)
            def _(h=h):
                q_copy(h, j, 0, other).wait_send()

            @pl.when(q_next[h][1])
            def _(h=h):
                q_copy(h, j, 1, q_next[h][0]).wait_send()

        return carry

    lax.fori_loop(0, Q_CHUNKS, drain_q, 0)

    def drain_c(i, carry):
        @pl.when(lead)
        def _():
            c_copy(i, 0, other, False).wait_send()

        @pl.when(top | (lead & (z == 1)))
        def _():
            c_copy(i, 1, z_up, False).wait_send()

        @pl.when(top)
        def _():
            c_copy(i, 2, z_down, False).wait_send()

        return carry

    lax.fori_loop(0, C_CHUNKS, drain_c, 0)


def panels(asm, g, inverses, strokes):
    rows, cols = asm.shape
    modes = strokes.shape[1]
    vmem = pl.BlockSpec(memory_space=VMEM)
    return pl.pallas_call(
        panel_kernel,
        out_shape=(VMEM((rows, cols), F32), VMEM((rows, modes), F32)),
        in_specs=[vmem] * 4,
        out_specs=(vmem, vmem),
        scratch_shapes=[
            VMEM((rows, 512), F32),
            VMEM((512, cols), F32),
            VMEM((512, 256), F32),
            VMEM((rows, 512), F32),
            VMEM((512, cols), F32),
            VMEM((512, cols), jnp.bfloat16),
            VMEM((512, cols), jnp.bfloat16),
            VMEM((512, modes), F32),
            VMEM((rows, modes), F32),
            VMEM((2, 4, rows // 8, modes), F32),
            VMEM((2, 3, rows // 32, modes), F32),
            DMA((4,)),
            DMA,
            DMA((4, P_CHUNKS)),
            DMA((4, P_CHUNKS)),
            DMA((2, Q_CHUNKS, 2)),
            DMA((2, Q_CHUNKS)),
            DMA((C_CHUNKS, 3)),
            DMA((C_CHUNKS,)),
            DMA((4, 2, 3)),
            DMA((4, 2, 3)),
        ],
        compiler_params=pltpu.CompilerParams(
            collective_id=1, has_side_effects=True, vmem_limit_bytes=32 << 20
        ),
        name="panels",
    )(resident(asm), resident(g), inverses, resident(strokes))


def on_device(far_field, inverses, test_table, trial_table, tile_list, tile_nodes, strokes):
    packed = make_pieces(tile_list, tile_nodes, test_table, trial_table, 16)
    arrived, far, g, held_strokes = exchange(packed, far_field, strokes)
    asm, g = place(arrived, far, g, held_strokes)
    return panels(asm, g, inverses, held_strokes)


def solution(mesh):
    return jax.shard_map(
        on_device,
        mesh=mesh,
        in_specs=(
            P("row", "col"),
            P(),
            P(("row", "col"), None),
            P(("row", "col"), None),
            P(("row", "col"), None),
            P(("row", "col"), None),
            P("col", None),
        ),
        out_specs=(P("row", "col"), P("row", None)),
        check_vma=False,
    )
```

```python
import jax
import jax.numpy as jnp
from jax import lax
from jax.experimental import pallas as pl
from jax.experimental.pallas import tpu as pltpu
from jax.sharding import PartitionSpec as P

MESH = pl.DeviceIdType.MESH
F32 = jnp.float32
VMEM = pltpu.VMEM
DMA = pltpu.SemaphoreType.DMA

LINK_TREE = (
    (0, 1, 2, 3), (1, 1, 1, 4), (3, 1, 1, 3), (3, 4, 3, 3),
    (0, 0, 4, 0), (1, 1, 0, 1), (3, 1, 0, 3), (0, 3, 0, 0),
    (0, 0, 2, 2), (0, 0, 2, 1), (0, 1, 2, 3), (0, 3, 2, 2),
    (4, 2, 2, 2), (2, 2, 2, 1), (2, 1, 1, 3), (2, 3, 3, 3),
)
TREE_DEPTH = (
    (0, 3, 4, 3, 1, 2, 3, 2, 2, 3, 4, 3, 3, 4, 5, 4),
    (0, 1, 2, 3, 3, 2, 3, 4, 4, 3, 4, 5, 3, 2, 3, 4),
    (0, 3, 4, 3, 3, 4, 5, 4, 2, 3, 4, 3, 1, 2, 3, 2),
    (0, 3, 2, 1, 3, 4, 3, 2, 4, 5, 4, 3, 3, 4, 3, 2),
)
STEPS_X = (1, 0, 3, 0)
STEPS_Y = (0, 1, 0, 3)


def table(values, index):
    found = jnp.int32(0)
    for at, value in enumerate(values):
        if value:
            found = found + jnp.where(index == at, jnp.int32(value), jnp.int32(0))
    return found


def mod4(value):
    return lax.rem(value, 4)


def split(a):
    high = a.astype(jnp.bfloat16)
    return high, (a - high.astype(F32)).astype(jnp.bfloat16)


def dot_split(a, b):
    def one(u, v):
        return jnp.dot(u, v, preferred_element_type=F32)

    return one(a[0], b[0]) + (one(a[0], b[1]) + one(a[1], b[0]))


def dot(a, b):
    return dot_split(split(a), split(b))


def pieces_kernel(
    tiles_hbm, nodes_hbm, test_hbm, trial_hbm, out_ref, test_ref, trial_ref, left, right, tiles_ref, nodes_ref,
    count, label, sem
):
    owned, quad = nodes_ref.shape
    dests = out_ref.shape[0]
    tile = test_ref.shape[1]
    block_cols = 8
    block_rows = 16
    loads = [
        pltpu.make_async_copy(src, dst, sem.at[n])
        for n, (src, dst) in enumerate(
            ((tiles_hbm, tiles_ref), (nodes_hbm, nodes_ref), (test_hbm, test_ref), (trial_hbm, trial_ref))
        )
    ]
    for load in loads:
        load.start()

    def clear(at, carry):
        count[at] = 0
        label[2 * at] = -1
        label[2 * at + 1] = -1
        return carry

    lax.fori_loop(0, dests, clear, 0)
    for load in loads:
        load.wait()
    sublane = lax.broadcasted_iota(jnp.int32, (8, tile), 0)

    def gather(t, slot):
        for q in range(0, quad, 8):
            nodes = [nodes_ref[t, q + k] for k in range(8)]
            for table_ref, to in ((test_ref, left), (trial_ref, right)):
                rows = [jnp.broadcast_to(table_ref[pl.ds(node, 1), :], (8, tile)) for node in nodes]
                for width in (1, 2, 4):
                    mask = lax.rem(sublane, 2 * width) < width
                    rows = [jnp.where(mask, rows[n], rows[n + 1]) for n in range(0, len(rows), 2)]
                to[slot, q : q + 8, :] = rows[0]

    def integrate(t, slot):
        piece = dot(left[slot].T, right[slot])
        block_row = lax.rem(tiles_ref[0, t], block_rows)
        block_col = tiles_ref[1, t]
        dest = lax.div(block_col, block_cols)
        place = count[dest]
        count[dest] = place + 1
        label[2 * dest + place] = block_row * block_cols + lax.rem(block_col, block_cols)
        out_ref[dest, pl.ds(pl.multiple_of(place * tile, tile), tile), :] = piece

    def two_tiles(n, carry):
        gather(2 * n + 1, 1)
        integrate(2 * n, 0)
        gather(2 * n + 2, 0)
        integrate(2 * n + 1, 1)
        return carry

    gather(0, 0)
    lax.fori_loop(0, owned // 2 - 1, two_tiles, 0)
    gather(owned - 1, 1)
    integrate(owned - 2, 0)
    integrate(owned - 1, 1)
    for d in range(dests):
        both = jnp.where(sublane == 0, label[2 * d], label[2 * d + 1])
        out_ref[d, 2 * tile : 2 * tile + 8, :] = both.astype(F32)


def make_pieces(tile_list, tile_nodes, test_table, trial_table, dests):
    tile = test_table.shape[1]
    quad = tile_nodes.shape[1]
    operands = (tile_list.T, tile_nodes, test_table, trial_table)
    return pl.pallas_call(
        pieces_kernel,
        out_shape=VMEM((dests, 2 * tile + 8, tile), F32),
        in_specs=[pl.BlockSpec(memory_space=pltpu.HBM)] * 4,
        out_specs=pl.BlockSpec(memory_space=VMEM),
        scratch_shapes=[
            VMEM(test_table.shape, F32),
            VMEM(trial_table.shape, F32),
            VMEM((2, quad, tile), F32),
            VMEM((2, quad, tile), F32),
            pltpu.SMEM(operands[0].shape, jnp.int32),
            pltpu.SMEM(tile_nodes.shape, jnp.int32),
            pltpu.SMEM((dests,), jnp.int32),
            pltpu.SMEM((2 * dests,), jnp.int32),
            DMA((4,)),
        ],
        compiler_params=pltpu.CompilerParams(vmem_limit_bytes=8 << 20),
        name="pieces",
    )(*(pltpu.with_memory_space_constraint(operand, pltpu.HBM) for operand in operands))


OFFSETS = sorted(
    ((dx, dy) for dx in range(4) for dy in range(4) if dx or dy),
    key=lambda o: min(o[0], 4 - o[0]) + min(o[1], 4 - o[1]),
)
FAR_PARTS = 8


def resident(array):
    return pltpu.with_memory_space_constraint(array, VMEM)


def exchange_kernel(packed, far_hbm, s_hbm, arrived, far, strokes, send_sem, recv_sem, own_sem, far_sem, s_sem):
    row = lax.axis_index("row")
    col = lax.axis_index("col")
    x, y = lax.div(col, 4), lax.rem(col, 4)
    peers = [mod4(x + dx) * 4 + mod4(y + dy) for dx, dy in OFFSETS]
    barrier = pltpu.get_barrier_semaphore()
    for peer in peers:
        pl.semaphore_signal(barrier, inc=1, device_id=(row, peer), device_id_type=MESH)
    size = far.shape[0] // FAR_PARTS
    load_s = pltpu.make_async_copy(s_hbm, strokes, s_sem)
    load_s.start()
    loads = []
    for j in range(FAR_PARTS):
        part = pl.ds(j * size, size)
        loads.append(pltpu.make_async_copy(far_hbm.at[part], far.at[part], far_sem.at[j]))
        loads[-1].start()
    pl.semaphore_wait(barrier, len(peers))
    copies = []
    for k, peer in enumerate(peers):
        copies.append(
            pltpu.make_async_remote_copy(
                src_ref=packed.at[peer],
                dst_ref=arrived.at[col],
                send_sem=send_sem.at[k],
                recv_sem=recv_sem.at[k],
                device_id=(row, peer),
                device_id_type=MESH,
            )
        )
        copies[-1].start()
    own = pltpu.make_async_copy(packed.at[col], arrived.at[col], own_sem)
    own.start()
    load_s.wait()
    for load in loads:
        load.wait()
    own.wait()
    for copy in copies:
        copy.wait()


def exchange(packed, far, strokes):
    n = len(OFFSETS)
    hbm = pl.BlockSpec(memory_space=pltpu.HBM)
    vmem = pl.BlockSpec(memory_space=VMEM)
    return pl.pallas_call(
        exchange_kernel,
        out_shape=(
            VMEM(packed.shape, F32),
            VMEM(far.shape, F32),
            VMEM(strokes.shape, F32),
        ),
        in_specs=[vmem, hbm, hbm],
        out_specs=(vmem,) * 3,
        scratch_shapes=[DMA((n,)), DMA((n,)), DMA, DMA((FAR_PARTS,)), DMA],
        compiler_params=pltpu.CompilerParams(
            collective_id=0, has_side_effects=True, vmem_limit_bytes=8 << 20
        ),
        name="exchange",
    )(
        resident(packed),
        pltpu.with_memory_space_constraint(far, pltpu.HBM),
        pltpu.with_memory_space_constraint(strokes, pltpu.HBM),
    )


def place_kernel(arrived, far, out, label):
    tile = arrived.shape[2]
    for d in range(arrived.shape[0]):
        for k in range(2):
            at = 2 * tile + k
            label[2 * d + k] = jnp.max(arrived[d, at : at + 1, :]).astype(jnp.int32)

    def add(s, carry):
        lab = label[s]

        @pl.when(lab >= 0)
        def _():
            rows = pl.ds(pl.multiple_of(lax.div(lab, 8) * tile, tile), tile)
            cols = pl.ds(pl.multiple_of(lax.rem(lab, 8) * tile, tile), tile)
            piece = arrived[lax.div(s, 2), pl.ds(pl.multiple_of(lax.rem(s, 2) * tile, tile), tile), :]
            out[rows, cols] = out[rows, cols] + piece

        return carry

    lax.fori_loop(0, label.shape[0], add, 0)


def place(arrived, far):
    vmem = pl.BlockSpec(memory_space=VMEM)
    return pl.pallas_call(
        place_kernel,
        out_shape=VMEM(far.shape, F32),
        in_specs=[vmem] * 2,
        out_specs=vmem,
        scratch_shapes=[pltpu.SMEM((2 * arrived.shape[0],), jnp.int32)],
        input_output_aliases={1: 0},
        compiler_params=pltpu.CompilerParams(vmem_limit_bytes=8 << 20),
        name="place",
    )(resident(arrived), resident(far))


P_CHUNKS = 16
P_ROWS = 128
Q_CHUNKS = 16
Q_ROWS = 32
C_CHUNKS = 4
LAG = 4
C_LAG = 2
G_STEP = 1


def panel_kernel(
    asm, inv_ref, s_ref, out_ref, img, g_ref, p_ref, q_ref, c_ref, l_ref, u_ref, u_high, u_low, us_ref,
    part, stage1, stage2, load_p, load_q, send_p, recv_p, send_q, recv_q, send_c, recv_c, send_i, recv_i
):
    row = lax.axis_index("row")
    col = lax.axis_index("col")
    x, y = lax.div(col, 4), lax.rem(col, 4)
    z, core = lax.div(row, 2), lax.rem(row, 2)
    source = col == 0
    top = row == 0
    z_up = mod4(z + 1) * 2 + core
    z_down = mod4(z + 3) * 2 + core
    other = z * 2 + 1 - core
    neighbours = [mod4(x + STEPS_X[d]) * 4 + mod4(y + STEPS_Y[d]) for d in range(4)]
    link_tree = [table([LINK_TREE[v][d] for v in range(16)], col) for d in range(4)]
    depth = [table(TREE_DEPTH[t], col) for t in range(4)]

    across = [mod4(x + k) * 4 + y for k in range(4)]
    along = [x * 4 + mod4(y + k) for k in range(4)]
    barrier = pltpu.get_barrier_semaphore()
    for k in range(1, 4):
        pl.semaphore_signal(barrier, inc=1, device_id=(row, across[k]), device_id_type=MESH)
        pl.semaphore_signal(barrier, inc=1, device_id=(row, along[k]), device_id_type=MESH)
    for r in (z_up, z_down, other):
        pl.semaphore_signal(barrier, inc=1, device_id=(r, col), device_id_type=MESH)

    quarter = p_ref.shape[0] // 4

    def load_quarter(k):
        rows = pl.ds(pl.multiple_of(k * quarter, quarter), quarter)
        return pltpu.make_async_copy(asm.at[rows, pl.ds(0, 512)], p_ref.at[rows, :], load_p.at[k])

    load_rows = pltpu.make_async_copy(asm.at[pl.ds(0, 512), :], q_ref, load_q)

    @pl.when(source)
    def _():
        for k in range(4):
            load_quarter(k).start()

    @pl.when(top)
    def _():
        load_rows.start()

    pl.semaphore_wait(barrier, 9)

    @pl.when(top)
    def _():
        load_rows.wait()

    def p_copy(t, i, d):
        at = p_ref.at[
            pl.ds(pl.multiple_of(i * P_ROWS, P_ROWS), P_ROWS), pl.ds(t * 128, 128)
        ]
        return pltpu.make_async_remote_copy(
            src_ref=at,
            dst_ref=at,
            send_sem=send_p.at[d, i],
            recv_sem=recv_p.at[t, i],
            device_id=(row, neighbours[d]),
            device_id_type=MESH,
        )

    def q_copy(h, j, way, r):
        at = q_ref.at[pl.ds(pl.multiple_of(j * Q_ROWS, Q_ROWS), Q_ROWS), pl.ds(h * 512, 512)]
        return pltpu.make_async_remote_copy(
            src_ref=at,
            dst_ref=at,
            send_sem=send_q.at[h, j, way],
            recv_sem=recv_q.at[h, j],
            device_id=(r, col),
            device_id_type=MESH,
        )

    def c_copy(i, way, r, first):
        rows = pl.ds(pl.multiple_of(i * P_ROWS, P_ROWS), P_ROWS)
        here = c_ref.at[rows, :]
        start = pl.multiple_of(jnp.where(i < C_CHUNKS // 2, 256, 0), 256)
        return pltpu.make_async_remote_copy(
            src_ref=p_ref.at[rows, pl.ds(start, 256)] if first else here,
            dst_ref=here,
            send_sem=send_c.at[i, way],
            recv_sem=recv_c.at[i],
            device_id=(r, col),
            device_id_type=MESH,
        )

    lead = core == 0
    q_depth = [z + core, mod4(4 - z) + core]
    q_next = [(z_up, lead & (z < 3)), (z_down, lead & (z != 1))]
    deepest = jnp.maximum(jnp.maximum(depth[0], depth[1]), jnp.maximum(depth[2], depth[3]))
    c_depth = 1 + LAG * deepest + C_LAG * (jnp.where(z == 2, 2, jnp.where(z == 0, 0, 1)) + core)
    big = out_ref.shape[0] // 8

    def step(s, carry):
        for t in range(4):
            i = s - LAG * depth[t]

            @pl.when((i >= 0) & (i < P_CHUNKS))
            def _(t=t, i=i):
                if t == 0:

                    @pl.when(source & (lax.rem(i, P_CHUNKS // 4) == 0))
                    def _():
                        load_quarter(lax.div(i, P_CHUNKS // 4)).wait()

                @pl.when(jnp.logical_not(source))
                def _():
                    p_copy(t, i, 0).wait_recv()

                for d in range(4):

                    @pl.when(link_tree[d] == t)
                    def _(d=d):
                        p_copy(t, i, d).start()

        for h in range(2):
            j = s - LAG * q_depth[h]

            @pl.when((j >= 0) & (j < Q_CHUNKS))
            def _(h=h, j=j):
                @pl.when(jnp.logical_not(top))
                def _():
                    q_copy(h, j, 0, other).wait_recv()

                @pl.when(lead)
                def _():
                    q_copy(h, j, 0, other).start()

                @pl.when(q_next[h][1])
                def _():
                    q_copy(h, j, 1, q_next[h][0]).start()

        i = s - c_depth

        @pl.when((i >= 0) & (i < C_CHUNKS))
        def _():
            @pl.when(top)
            def _():
                c_copy(i, 0, other, True).start()
                c_copy(i, 1, z_up, True).start()
                c_copy(i, 2, z_down, True).start()

            @pl.when(jnp.logical_not(top))
            def _():
                c_copy(i, 0, other, False).wait_recv()

                @pl.when(lead)
                def _():
                    c_copy(i, 0, other, False).start()

                @pl.when(lead & (z == 1))
                def _():
                    c_copy(i, 1, z_up, False).start()

        n = s - G_STEP

        @pl.when((n >= 0) & (n < 8))
        def _():
            mine = pl.ds(pl.multiple_of(n * big, big), big)
            g_ref[mine, :] = dot(asm[mine, :], s_ref[...])

        return carry

    lax.fori_loop(0, max(P_CHUNKS + 5 * LAG, C_CHUNKS + 1 + 5 * LAG + 3 * C_LAG), step, 0)

    @pl.when(top)
    def _():
        c_ref[0:256, :] = p_ref[0:256, 256:512]
        c_ref[256:512, :] = p_ref[256:512, 0:256]

    inv0, inv1 = split(inv_ref[0]), split(inv_ref[1])
    upper0 = q_ref[0:256, :]
    ratio = dot_split(split(c_ref[256:512, :]), inv0)
    u_ref[0:256, :] = upper0
    u_ref[256:512, :] = q_ref[256:512, :] - dot(ratio, upper0)

    @pl.when(source)
    def _():
        u_ref[0:256, 0:256] = jnp.zeros((256, 256), F32)
        u_ref[256:512, 0:512] = jnp.zeros((256, 512), F32)

    u_high[...], u_low[...] = split(u_ref[...])
    us_ref[...] = dot_split((u_high[...], u_low[...]), split(s_ref[...]))

    rows = part.shape[0]
    half = rows // 2
    small = big // 4
    outer = (x, y)
    inner = (y, x)
    outer_peers = (across, along)
    inner_peers = (along, across)

    def at(start, count):
        return pl.ds(pl.multiple_of(start, count), count)

    def remote(src, dst, stage, h, k, peer):
        return pltpu.make_async_remote_copy(
            src_ref=src,
            dst_ref=dst,
            send_sem=send_i.at[stage, h, k - 1],
            recv_sem=recv_i.at[stage, h, k - 1],
            device_id=(row, peer),
            device_id_type=MESH,
        )

    def first_copy(h, k):
        to = mod4(outer[h] + k)
        peer = to * 4 + y if h == 0 else x * 4 + to
        return remote(part.at[at(h * half + to * big, big), :], stage1.at[h, k - 1], 0, h, k, peer)

    def finish_tile(j, carry):
        mine = at(j * big, big)
        lower = l_ref[mine, :]
        out_ref[mine, :] = asm[mine, :] - dot_split(split(lower), (u_high[...], u_low[...]))

        @pl.when(source & ((row > 0) | (j > 0)))
        def _():
            out_ref[mine, 0:256] = l_ref[mine, 0:256]

        @pl.when(source & ((row > 0) | (j > 1)))
        def _():
            out_ref[mine, 256:512] = l_ref[mine, 256:512]

        return carry

    def two_tiles(n, carry):
        k = table((2, 1, 3, 0), n)
        tiles = []
        for h in range(2):
            j = h * 4 + mod4(outer[h] + k)
            tiles.append((at(j * big, big), (row > 0) | (j > 0), (row > 0) | (j > 1)))
        lower0 = [jnp.where(b0, dot_split(split(p_ref[m, 0:256]), inv0), 0.0) for m, b0, _ in tiles]
        beside = split(c_ref[0:256, :])
        rest = [p_ref[m, 256:512] - dot_split(split(low), beside) for (m, _, _), low in zip(tiles, lower0)]
        lower1 = [jnp.where(b1, dot_split(split(r), inv1), 0.0) for (_, _, b1), r in zip(tiles, rest)]
        us0, us1 = split(us_ref[0:256, :]), split(us_ref[256:512, :])
        for (m, _, _), low0, low1 in zip(tiles, lower0, lower1):
            l_ref[m, 0:256] = low0
            l_ref[m, 256:512] = low1
            part[m, :] = g_ref[m, :] - (dot_split(split(low0), us0) + dot_split(split(low1), us1))

        @pl.when(source)
        def _():
            for m, b0, b1 in tiles:
                low0, low1 = l_ref[m, 0:256], l_ref[m, 256:512]
                left = p_ref[m, 256:512] - dot(low0, c_ref[0:256, :])
                change0 = jnp.where(b0, low0 - p_ref[m, 0:256], 0.0)
                change1 = jnp.where(b1, low1 - left, 0.0)
                part[m, :] += dot(change0, s_ref[0:256, :]) + dot(change1, s_ref[256:512, :])

        @pl.when(k > 0)
        def _():
            for h in range(2):
                first_copy(h, k).start()

        return carry

    lax.fori_loop(0, 4, two_tiles, 0)

    order = (2, 1, 3)
    second, third, fourth = [], [], []
    for h in range(2):
        for k in order:
            first_copy(h, k).wait_recv()
        total = part[at(h * half + outer[h] * big, big), :]
        for k in range(1, 4):
            total = total + stage1[h, k - 1]
        stage1[h, 3] = total
        for k in order:
            to = mod4(inner[h] + k)
            copy = remote(
                stage1.at[h, 3, at(to * small, small), :], stage2.at[h, k - 1], 1, h, k, inner_peers[h][k]
            )
            copy.start()
            second.append((h, copy))
    lax.fori_loop(0, 2, finish_tile, 0)
    for h in range(2):
        for g, copy in second:
            if g == h:
                copy.wait_recv()
        total = stage1[h, 3, at(inner[h] * small, small), :]
        for k in range(1, 4):
            total = total + stage2[h, k - 1]
        mine = at(h * half + outer[h] * big + inner[h] * small, small)
        img[mine, :] = total
        for k in order:
            copy = remote(img.at[mine, :], img.at[mine, :], 2, h, k, inner_peers[h][k])
            copy.start()
            third.append((h, copy))
    lax.fori_loop(2, 4, finish_tile, 0)
    for h in range(2):
        for g, copy in third:
            if g == h:
                copy.wait_recv()
        mine = at(h * half + outer[h] * big, big)
        for k in order:
            copy = remote(img.at[mine, :], img.at[mine, :], 3, h, k, outer_peers[h][k])
            copy.start()
            fourth.append((h, copy))
    lax.fori_loop(4, 8, finish_tile, 0)
    for _, copy in fourth:
        copy.wait_recv()
    for h in range(2):
        for k in order:
            first_copy(h, k).wait_send()
    for _, copy in second + third + fourth:
        copy.wait_send()
    def drain_p(i, carry):
        for d in range(4):

            @pl.when(link_tree[d] < 4)
            def _(d=d):
                p_copy(0, i, d).wait_send()

        return carry

    lax.fori_loop(0, P_CHUNKS, drain_p, 0)

    def drain_q(j, carry):
        for h in range(2):

            @pl.when(lead)
            def _(h=h):
                q_copy(h, j, 0, other).wait_send()

            @pl.when(q_next[h][1])
            def _(h=h):
                q_copy(h, j, 1, q_next[h][0]).wait_send()

        return carry

    lax.fori_loop(0, Q_CHUNKS, drain_q, 0)

    def drain_c(i, carry):
        @pl.when(lead)
        def _():
            c_copy(i, 0, other, False).wait_send()

        @pl.when(top | (lead & (z == 1)))
        def _():
            c_copy(i, 1, z_up, False).wait_send()

        @pl.when(top)
        def _():
            c_copy(i, 2, z_down, False).wait_send()

        return carry

    lax.fori_loop(0, C_CHUNKS, drain_c, 0)


def panels(asm, inverses, strokes):
    rows, cols = asm.shape
    modes = strokes.shape[1]
    vmem = pl.BlockSpec(memory_space=VMEM)
    return pl.pallas_call(
        panel_kernel,
        out_shape=(VMEM((rows, cols), F32), VMEM((rows, modes), F32)),
        in_specs=[vmem] * 3,
        out_specs=(vmem, vmem),
        scratch_shapes=[
            VMEM((rows, modes), F32),
            VMEM((rows, 512), F32),
            VMEM((512, cols), F32),
            VMEM((512, 256), F32),
            VMEM((rows, 512), F32),
            VMEM((512, cols), F32),
            VMEM((512, cols), jnp.bfloat16),
            VMEM((512, cols), jnp.bfloat16),
            VMEM((512, modes), F32),
            VMEM((rows, modes), F32),
            VMEM((2, 4, rows // 8, modes), F32),
            VMEM((2, 3, rows // 32, modes), F32),
            DMA((4,)),
            DMA,
            DMA((4, P_CHUNKS)),
            DMA((4, P_CHUNKS)),
            DMA((2, Q_CHUNKS, 2)),
            DMA((2, Q_CHUNKS)),
            DMA((C_CHUNKS, 3)),
            DMA((C_CHUNKS,)),
            DMA((4, 2, 3)),
            DMA((4, 2, 3)),
        ],
        compiler_params=pltpu.CompilerParams(
            collective_id=1, has_side_effects=True, vmem_limit_bytes=32 << 20
        ),
        name="panels",
    )(resident(asm), inverses, resident(strokes))


def hand_out_kernel(factored, image, factored_out, image_out, sem):
    rows = factored.shape[0] // 4
    copies = [
        pltpu.make_async_copy(src.at[pl.ds(n * rows, rows)], dst.at[pl.ds(n * rows, rows)], sem.at[which, n])
        for which, (src, dst) in enumerate(((factored, factored_out), (image, image_out)))
        for n in range(4)
    ]
    for copy in copies:
        copy.start()
    for copy in copies:
        copy.wait()


def hand_out(factored, image):
    vmem = pl.BlockSpec(memory_space=VMEM)
    hbm = pl.BlockSpec(memory_space=pltpu.HBM)
    return pl.pallas_call(
        hand_out_kernel,
        out_shape=(pltpu.HBM(factored.shape, F32), pltpu.HBM(image.shape, F32)),
        in_specs=[vmem] * 2,
        out_specs=(hbm, hbm),
        scratch_shapes=[DMA((2, 4))],
        compiler_params=pltpu.CompilerParams(vmem_limit_bytes=8 << 20),
        name="hand_out",
    )(resident(factored), resident(image))


def on_device(far_field, inverses, test_table, trial_table, tile_list, tile_nodes, strokes):
    packed = make_pieces(tile_list, tile_nodes, test_table, trial_table, 16)
    arrived, far, held_strokes = exchange(packed, far_field, strokes)
    asm = place(arrived, far)
    return hand_out(*panels(asm, inverses, held_strokes))


def solution(mesh):
    return jax.shard_map(
        on_device,
        mesh=mesh,
        in_specs=(
            P("row", "col"),
            P(),
            P(("row", "col"), None),
            P(("row", "col"), None),
            P(("row", "col"), None),
            P(("row", "col"), None),
            P("col", None),
        ),
        out_specs=(P("row", "col"), P("row", None)),
        check_vma=False,
    )
```

```python
import jax
import jax.numpy as jnp
from jax import lax
from jax.experimental import pallas as pl
from jax.experimental.pallas import tpu as pltpu
from jax.sharding import PartitionSpec as P

MESH = pl.DeviceIdType.MESH
F32 = jnp.float32
VMEM = pltpu.VMEM
DMA = pltpu.SemaphoreType.DMA

LINK_TREE = (
    (0, 1, 2, 3), (1, 1, 1, 4), (3, 1, 1, 3), (3, 4, 3, 3),
    (0, 0, 4, 0), (1, 1, 0, 1), (3, 1, 0, 3), (0, 3, 0, 0),
    (0, 0, 2, 2), (0, 0, 2, 1), (0, 1, 2, 3), (0, 3, 2, 2),
    (4, 2, 2, 2), (2, 2, 2, 1), (2, 1, 1, 3), (2, 3, 3, 3),
)
TREE_DEPTH = (
    (0, 3, 4, 3, 1, 2, 3, 2, 2, 3, 4, 3, 3, 4, 5, 4),
    (0, 1, 2, 3, 3, 2, 3, 4, 4, 3, 4, 5, 3, 2, 3, 4),
    (0, 3, 4, 3, 3, 4, 5, 4, 2, 3, 4, 3, 1, 2, 3, 2),
    (0, 3, 2, 1, 3, 4, 3, 2, 4, 5, 4, 3, 3, 4, 3, 2),
)
STEPS_X = (1, 0, 3, 0)
STEPS_Y = (0, 1, 0, 3)


def table(values, index):
    found = jnp.int32(0)
    for at, value in enumerate(values):
        if value:
            found = found + jnp.where(index == at, jnp.int32(value), jnp.int32(0))
    return found


def mod4(value):
    return lax.rem(value, 4)


def split(a):
    high = a.astype(jnp.bfloat16)
    return high, (a - high.astype(F32)).astype(jnp.bfloat16)


def dot_split(a, b):
    def one(u, v):
        return jnp.dot(u, v, preferred_element_type=F32)

    return one(a[0], b[0]) + (one(a[0], b[1]) + one(a[1], b[0]))


def dot(a, b):
    return dot_split(split(a), split(b))


def pieces_kernel(
    tiles_hbm, nodes_hbm, test_hbm, trial_hbm, out_ref, test_ref, trial_ref, left, right, tiles_ref, nodes_ref,
    count, label, sem
):
    owned, quad = nodes_ref.shape
    dests = out_ref.shape[0]
    tile = test_ref.shape[1]
    block_cols = 8
    block_rows = 16
    loads = [
        pltpu.make_async_copy(src, dst, sem.at[n])
        for n, (src, dst) in enumerate(
            ((tiles_hbm, tiles_ref), (nodes_hbm, nodes_ref), (test_hbm, test_ref), (trial_hbm, trial_ref))
        )
    ]
    for load in loads:
        load.start()

    def clear(at, carry):
        count[at] = 0
        label[2 * at] = -1
        label[2 * at + 1] = -1
        return carry

    lax.fori_loop(0, dests, clear, 0)
    for load in loads:
        load.wait()
    sublane = lax.broadcasted_iota(jnp.int32, (8, tile), 0)

    def gather(t, slot):
        for q in range(0, quad, 8):
            nodes = [nodes_ref[t, q + k] for k in range(8)]
            for table_ref, to in ((test_ref, left), (trial_ref, right)):
                rows = [jnp.broadcast_to(table_ref[pl.ds(node, 1), :], (8, tile)) for node in nodes]
                for width in (1, 2, 4):
                    mask = lax.rem(sublane, 2 * width) < width
                    rows = [jnp.where(mask, rows[n], rows[n + 1]) for n in range(0, len(rows), 2)]
                to[slot, q : q + 8, :] = rows[0]

    def integrate(t, slot):
        piece = dot(left[slot].T, right[slot])
        block_row = lax.rem(tiles_ref[0, t], block_rows)
        block_col = tiles_ref[1, t]
        dest = lax.div(block_col, block_cols)
        place = count[dest]
        count[dest] = place + 1
        label[2 * dest + place] = block_row * block_cols + lax.rem(block_col, block_cols)
        out_ref[dest, pl.ds(pl.multiple_of(place * tile, tile), tile), :] = piece

    def two_tiles(n, carry):
        gather(2 * n + 1, 1)
        integrate(2 * n, 0)
        gather(2 * n + 2, 0)
        integrate(2 * n + 1, 1)
        return carry

    gather(0, 0)
    lax.fori_loop(0, owned // 2 - 1, two_tiles, 0)
    gather(owned - 1, 1)
    integrate(owned - 2, 0)
    integrate(owned - 1, 1)
    for d in range(dests):
        both = jnp.where(sublane == 0, label[2 * d], label[2 * d + 1])
        out_ref[d, 2 * tile : 2 * tile + 8, :] = both.astype(F32)


def make_pieces(tile_list, tile_nodes, test_table, trial_table, dests):
    tile = test_table.shape[1]
    quad = tile_nodes.shape[1]
    operands = (tile_list.T, tile_nodes, test_table, trial_table)
    return pl.pallas_call(
        pieces_kernel,
        out_shape=VMEM((dests, 2 * tile + 8, tile), F32),
        in_specs=[pl.BlockSpec(memory_space=pltpu.HBM)] * 4,
        out_specs=pl.BlockSpec(memory_space=VMEM),
        scratch_shapes=[
            VMEM(test_table.shape, F32),
            VMEM(trial_table.shape, F32),
            VMEM((2, quad, tile), F32),
            VMEM((2, quad, tile), F32),
            pltpu.SMEM(operands[0].shape, jnp.int32),
            pltpu.SMEM(tile_nodes.shape, jnp.int32),
            pltpu.SMEM((dests,), jnp.int32),
            pltpu.SMEM((2 * dests,), jnp.int32),
            DMA((4,)),
        ],
        compiler_params=pltpu.CompilerParams(vmem_limit_bytes=8 << 20),
        name="pieces",
    )(*(pltpu.with_memory_space_constraint(operand, pltpu.HBM) for operand in operands))


OFFSETS = sorted(
    ((dx, dy) for dx in range(4) for dy in range(4) if dx or dy),
    key=lambda o: min(o[0], 4 - o[0]) + min(o[1], 4 - o[1]),
)
FAR_PARTS = 8


def resident(array):
    return pltpu.with_memory_space_constraint(array, VMEM)


def exchange_kernel(packed, far_hbm, s_hbm, arrived, far, strokes, send_sem, recv_sem, own_sem, far_sem, s_sem):
    row = lax.axis_index("row")
    col = lax.axis_index("col")
    x, y = lax.div(col, 4), lax.rem(col, 4)
    peers = [mod4(x + dx) * 4 + mod4(y + dy) for dx, dy in OFFSETS]
    barrier = pltpu.get_barrier_semaphore()
    for peer in peers:
        pl.semaphore_signal(barrier, inc=1, device_id=(row, peer), device_id_type=MESH)
    size = far.shape[0] // FAR_PARTS
    load_s = pltpu.make_async_copy(s_hbm, strokes, s_sem)
    load_s.start()
    loads = []
    for j in range(FAR_PARTS):
        part = pl.ds(j * size, size)
        loads.append(pltpu.make_async_copy(far_hbm.at[part], far.at[part], far_sem.at[j]))
        loads[-1].start()
    pl.semaphore_wait(barrier, len(peers))
    copies = []
    for k, peer in enumerate(peers):
        copies.append(
            pltpu.make_async_remote_copy(
                src_ref=packed.at[peer],
                dst_ref=arrived.at[col],
                send_sem=send_sem.at[k],
                recv_sem=recv_sem.at[k],
                device_id=(row, peer),
                device_id_type=MESH,
            )
        )
        copies[-1].start()
    own = pltpu.make_async_copy(packed.at[col], arrived.at[col], own_sem)
    own.start()
    load_s.wait()
    for load in loads:
        load.wait()
    own.wait()
    for copy in copies:
        copy.wait()


def exchange(packed, far, strokes):
    n = len(OFFSETS)
    hbm = pl.BlockSpec(memory_space=pltpu.HBM)
    vmem = pl.BlockSpec(memory_space=VMEM)
    return pl.pallas_call(
        exchange_kernel,
        out_shape=(
            VMEM(packed.shape, F32),
            VMEM(far.shape, F32),
            VMEM(strokes.shape, F32),
        ),
        in_specs=[vmem, hbm, hbm],
        out_specs=(vmem,) * 3,
        scratch_shapes=[DMA((n,)), DMA((n,)), DMA, DMA((FAR_PARTS,)), DMA],
        compiler_params=pltpu.CompilerParams(
            collective_id=0, has_side_effects=True, vmem_limit_bytes=8 << 20
        ),
        name="exchange",
    )(
        resident(packed),
        pltpu.with_memory_space_constraint(far, pltpu.HBM),
        pltpu.with_memory_space_constraint(strokes, pltpu.HBM),
    )


def place_kernel(arrived, far, out, label):
    tile = arrived.shape[2]
    for d in range(arrived.shape[0]):
        for k in range(2):
            at = 2 * tile + k
            label[2 * d + k] = jnp.max(arrived[d, at : at + 1, :]).astype(jnp.int32)

    def add(s, carry):
        lab = label[s]

        @pl.when(lab >= 0)
        def _():
            rows = pl.ds(pl.multiple_of(lax.div(lab, 8) * tile, tile), tile)
            cols = pl.ds(pl.multiple_of(lax.rem(lab, 8) * tile, tile), tile)
            piece = arrived[lax.div(s, 2), pl.ds(pl.multiple_of(lax.rem(s, 2) * tile, tile), tile), :]
            out[rows, cols] = out[rows, cols] + piece

        return carry

    lax.fori_loop(0, label.shape[0], add, 0)


def place(arrived, far):
    vmem = pl.BlockSpec(memory_space=VMEM)
    return pl.pallas_call(
        place_kernel,
        out_shape=VMEM(far.shape, F32),
        in_specs=[vmem] * 2,
        out_specs=vmem,
        scratch_shapes=[pltpu.SMEM((2 * arrived.shape[0],), jnp.int32)],
        input_output_aliases={1: 0},
        compiler_params=pltpu.CompilerParams(vmem_limit_bytes=8 << 20),
        name="place",
    )(resident(arrived), resident(far))


P_CHUNKS = 16
P_ROWS = 128
Q_CHUNKS = 16
Q_ROWS = 32
C_CHUNKS = 4
LAG = 4
C_LAG = 2
G_STEP = 1


def panel_kernel(
    asm, inv_ref, s_ref, out_ref, img, g_ref, p_ref, q_ref, c_ref, l_ref, u_ref, u_high, u_low, us_ref,
    part, stage1, stage2, load_p, load_q, send_p, recv_p, send_q, recv_q, send_c, recv_c, send1, recv1, send2, recv2,
    send3, recv3, send4, recv4
):
    row = lax.axis_index("row")
    col = lax.axis_index("col")
    x, y = lax.div(col, 4), lax.rem(col, 4)
    z, core = lax.div(row, 2), lax.rem(row, 2)
    source = col == 0
    top = row == 0
    z_up = mod4(z + 1) * 2 + core
    z_down = mod4(z + 3) * 2 + core
    other = z * 2 + 1 - core
    neighbours = [mod4(x + STEPS_X[d]) * 4 + mod4(y + STEPS_Y[d]) for d in range(4)]
    link_tree = [table([LINK_TREE[v][d] for v in range(16)], col) for d in range(4)]
    depth = [table(TREE_DEPTH[t], col) for t in range(4)]

    across = [mod4(x + k) * 4 + y for k in range(4)]
    along = [x * 4 + mod4(y + k) for k in range(4)]
    barrier = pltpu.get_barrier_semaphore()
    for k in range(1, 4):
        pl.semaphore_signal(barrier, inc=1, device_id=(row, across[k]), device_id_type=MESH)
        pl.semaphore_signal(barrier, inc=1, device_id=(row, along[k]), device_id_type=MESH)
    for r in (z_up, z_down, other):
        pl.semaphore_signal(barrier, inc=1, device_id=(r, col), device_id_type=MESH)

    quarter = p_ref.shape[0] // 4

    def load_quarter(k):
        rows = pl.ds(pl.multiple_of(k * quarter, quarter), quarter)
        return pltpu.make_async_copy(asm.at[rows, pl.ds(0, 512)], p_ref.at[rows, :], load_p.at[k])

    load_rows = pltpu.make_async_copy(asm.at[pl.ds(0, 512), :], q_ref, load_q)

    @pl.when(source)
    def _():
        for k in range(4):
            load_quarter(k).start()

    @pl.when(top)
    def _():
        load_rows.start()

    pl.semaphore_wait(barrier, 9)

    @pl.when(top)
    def _():
        load_rows.wait()

    def p_copy(t, i, d):
        at = p_ref.at[
            pl.ds(pl.multiple_of(i * P_ROWS, P_ROWS), P_ROWS), pl.ds(t * 128, 128)
        ]
        return pltpu.make_async_remote_copy(
            src_ref=at,
            dst_ref=at,
            send_sem=send_p.at[d, i],
            recv_sem=recv_p.at[t, i],
            device_id=(row, neighbours[d]),
            device_id_type=MESH,
        )

    def q_copy(h, j, way, r):
        at = q_ref.at[pl.ds(pl.multiple_of(j * Q_ROWS, Q_ROWS), Q_ROWS), pl.ds(h * 512, 512)]
        return pltpu.make_async_remote_copy(
            src_ref=at,
            dst_ref=at,
            send_sem=send_q.at[h, j, way],
            recv_sem=recv_q.at[h, j],
            device_id=(r, col),
            device_id_type=MESH,
        )

    def c_copy(i, way, r, first):
        rows = pl.ds(pl.multiple_of(i * P_ROWS, P_ROWS), P_ROWS)
        here = c_ref.at[rows, :]
        start = pl.multiple_of(jnp.where(i < C_CHUNKS // 2, 256, 0), 256)
        return pltpu.make_async_remote_copy(
            src_ref=p_ref.at[rows, pl.ds(start, 256)] if first else here,
            dst_ref=here,
            send_sem=send_c.at[i, way],
            recv_sem=recv_c.at[i],
            device_id=(r, col),
            device_id_type=MESH,
        )

    lead = core == 0
    q_depth = [z + core, mod4(4 - z) + core]
    q_next = [(z_up, lead & (z < 3)), (z_down, lead & (z != 1))]
    deepest = jnp.maximum(jnp.maximum(depth[0], depth[1]), jnp.maximum(depth[2], depth[3]))
    c_depth = 1 + LAG * deepest + C_LAG * (jnp.where(z == 2, 2, jnp.where(z == 0, 0, 1)) + core)
    big = out_ref.shape[0] // 8

    def step(s, carry):
        for t in range(4):
            i = s - LAG * depth[t]

            @pl.when((i >= 0) & (i < P_CHUNKS))
            def _(t=t, i=i):
                if t == 0:

                    @pl.when(source & (lax.rem(i, P_CHUNKS // 4) == 0))
                    def _():
                        load_quarter(lax.div(i, P_CHUNKS // 4)).wait()

                @pl.when(jnp.logical_not(source))
                def _():
                    p_copy(t, i, 0).wait_recv()

                for d in range(4):

                    @pl.when(link_tree[d] == t)
                    def _(d=d):
                        p_copy(t, i, d).start()

        for h in range(2):
            j = s - LAG * q_depth[h]

            @pl.when((j >= 0) & (j < Q_CHUNKS))
            def _(h=h, j=j):
                @pl.when(jnp.logical_not(top))
                def _():
                    q_copy(h, j, 0, other).wait_recv()

                @pl.when(lead)
                def _():
                    q_copy(h, j, 0, other).start()

                @pl.when(q_next[h][1])
                def _():
                    q_copy(h, j, 1, q_next[h][0]).start()

        i = s - c_depth

        @pl.when((i >= 0) & (i < C_CHUNKS))
        def _():
            @pl.when(top)
            def _():
                c_copy(i, 0, other, True).start()
                c_copy(i, 1, z_up, True).start()
                c_copy(i, 2, z_down, True).start()

            @pl.when(jnp.logical_not(top))
            def _():
                c_copy(i, 0, other, False).wait_recv()

                @pl.when(lead)
                def _():
                    c_copy(i, 0, other, False).start()

                @pl.when(lead & (z == 1))
                def _():
                    c_copy(i, 1, z_up, False).start()

        n = s - G_STEP

        @pl.when((n >= 0) & (n < 8))
        def _():
            mine = pl.ds(pl.multiple_of(n * big, big), big)
            g_ref[mine, :] = dot(asm[mine, :], s_ref[...])

        return carry

    lax.fori_loop(0, max(P_CHUNKS + 5 * LAG, C_CHUNKS + 1 + 5 * LAG + 3 * C_LAG), step, 0)

    @pl.when(top)
    def _():
        c_ref[0:256, :] = p_ref[0:256, 256:512]
        c_ref[256:512, :] = p_ref[256:512, 0:256]

    inv0, inv1 = split(inv_ref[0]), split(inv_ref[1])
    upper0 = q_ref[0:256, :]
    ratio = dot_split(split(c_ref[256:512, :]), inv0)
    u_ref[0:256, :] = upper0
    u_ref[256:512, :] = q_ref[256:512, :] - dot(ratio, upper0)

    @pl.when(source)
    def _():
        u_ref[0:256, 0:256] = jnp.zeros((256, 256), F32)
        u_ref[256:512, 0:512] = jnp.zeros((256, 512), F32)

    u_high[...], u_low[...] = split(u_ref[...])
    us_ref[...] = dot_split((u_high[...], u_low[...]), split(s_ref[...]))

    rows = part.shape[0]
    half = rows // 2
    small = big // 4
    outer = (x, y)
    inner = (y, x)
    outer_peers = (across, along)
    inner_peers = (along, across)

    def at(start, count):
        return pl.ds(pl.multiple_of(start, count), count)

    def remote(src, dst, send, recv, peer):
        return pltpu.make_async_remote_copy(
            src_ref=src, dst_ref=dst, send_sem=send, recv_sem=recv, device_id=(row, peer), device_id_type=MESH
        )

    def piece(h, m):
        return at(mod4(inner[h] + m) * small, small)

    def second_copy(h, m):
        return remote(
            stage1.at[h, 3, piece(h, m), :],
            stage2.at[h, m - 1],
            send2.at[h, m - 1],
            recv2.at[h, m - 1],
            inner_peers[h][m],
        )

    def third_copy(h, m):
        here = img.at[at(h * half + outer[h] * big + inner[h] * small, small), :]
        return remote(here, here, send3.at[h, m - 1], recv3.at[h, m - 1], inner_peers[h][m])

    def fourth_copy(h, k, m):
        here = img.at[at(h * half + outer[h] * big + mod4(inner[h] + 4 - m) * small, small), :]
        return remote(here, here, send4.at[h, k - 1, m], recv4.at[h, k - 1, m], outer_peers[h][k])

    def finish_tile(j, carry):
        mine = at(j * big, big)
        lower = l_ref[mine, :]
        out_ref[mine, :] = asm[mine, :] - dot_split(split(lower), (u_high[...], u_low[...]))

        @pl.when(source & ((row > 0) | (j > 0)))
        def _():
            out_ref[mine, 0:256] = l_ref[mine, 0:256]

        @pl.when(source & ((row > 0) | (j > 1)))
        def _():
            out_ref[mine, 256:512] = l_ref[mine, 256:512]

        return carry

    order = (2, 1, 3)
    pieces = (2, 1, 3, 0)

    def first_copy(h, k, m):
        to = mod4(outer[h] + k)
        return remote(
            part.at[at(h * half + to * big + mod4(inner[h] + m) * small, small), :],
            stage1.at[h, k - 1, piece(h, m), :],
            send1.at[h, k - 1, m],
            recv1.at[h, k - 1, m],
            to * 4 + y if h == 0 else x * 4 + to,
        )

    def two_tiles(n, carry):
        k = table((2, 1, 3, 0), n)
        tiles = []
        for h in range(2):
            j = h * 4 + mod4(outer[h] + k)
            tiles.append((at(j * big, big), (row > 0) | (j > 0), (row > 0) | (j > 1)))
        lower0 = [jnp.where(b0, dot_split(split(p_ref[m, 0:256]), inv0), 0.0) for m, b0, _ in tiles]
        beside = split(c_ref[0:256, :])
        rest = [p_ref[m, 256:512] - dot_split(split(low), beside) for (m, _, _), low in zip(tiles, lower0)]
        lower1 = [jnp.where(b1, dot_split(split(r), inv1), 0.0) for (_, _, b1), r in zip(tiles, rest)]
        us0, us1 = split(us_ref[0:256, :]), split(us_ref[256:512, :])
        for (m, _, _), low0, low1 in zip(tiles, lower0, lower1):
            l_ref[m, 0:256] = low0
            l_ref[m, 256:512] = low1
            part[m, :] = g_ref[m, :] - (dot_split(split(low0), us0) + dot_split(split(low1), us1))

        @pl.when(source)
        def _():
            for m, b0, b1 in tiles:
                low0, low1 = l_ref[m, 0:256], l_ref[m, 256:512]
                left = p_ref[m, 256:512] - dot(low0, c_ref[0:256, :])
                change0 = jnp.where(b0, low0 - p_ref[m, 0:256], 0.0)
                change1 = jnp.where(b1, low1 - left, 0.0)
                part[m, :] += dot(change0, s_ref[0:256, :]) + dot(change1, s_ref[256:512, :])

        @pl.when(k > 0)
        def _():
            for m in pieces:
                for h in range(2):
                    first_copy(h, k, m).start()

        return carry

    lax.fori_loop(0, 4, two_tiles, 0)

    for m in pieces:
        for h in range(2):
            for k in order:
                first_copy(h, k, m).wait_recv()
            total = part[at(h * half + outer[h] * big + mod4(inner[h] + m) * small, small), :]
            for k in range(1, 4):
                total = total + stage1[h, k - 1, piece(h, m), :]
            stage1[h, 3, piece(h, m), :] = total
            if m:
                second_copy(h, m).start()
    lax.fori_loop(0, 2, finish_tile, 0)
    for h in range(2):
        for m in order:
            second_copy(h, m).wait_recv()
        total = stage1[h, 3, piece(h, 0), :]
        for m in range(1, 4):
            total = total + stage2[h, m - 1]
        img[at(h * half + outer[h] * big + inner[h] * small, small), :] = total
        for m in order:
            third_copy(h, m).start()
        for k in order:
            fourth_copy(h, k, 0).start()
    lax.fori_loop(2, 4, finish_tile, 0)
    for m in (1, 3, 2):
        for h in range(2):
            third_copy(h, m).wait_recv()
            for k in order:
                fourth_copy(h, k, m).start()
    lax.fori_loop(4, 8, finish_tile, 0)
    for h in range(2):
        for k in order:
            for m in range(4):
                fourth_copy(h, k, m).wait_recv()
    for h in range(2):
        for k in order:
            second_copy(h, k).wait_send()
            third_copy(h, k).wait_send()
            for m in range(4):
                first_copy(h, k, m).wait_send()
                fourth_copy(h, k, m).wait_send()

    def drain_p(i, carry):
        for d in range(4):

            @pl.when(link_tree[d] < 4)
            def _(d=d):
                p_copy(0, i, d).wait_send()

        return carry

    lax.fori_loop(0, P_CHUNKS, drain_p, 0)

    def drain_q(j, carry):
        for h in range(2):

            @pl.when(lead)
            def _(h=h):
                q_copy(h, j, 0, other).wait_send()

            @pl.when(q_next[h][1])
            def _(h=h):
                q_copy(h, j, 1, q_next[h][0]).wait_send()

        return carry

    lax.fori_loop(0, Q_CHUNKS, drain_q, 0)

    def drain_c(i, carry):
        @pl.when(lead)
        def _():
            c_copy(i, 0, other, False).wait_send()

        @pl.when(top | (lead & (z == 1)))
        def _():
            c_copy(i, 1, z_up, False).wait_send()

        @pl.when(top)
        def _():
            c_copy(i, 2, z_down, False).wait_send()

        return carry

    lax.fori_loop(0, C_CHUNKS, drain_c, 0)


def panels(asm, inverses, strokes):
    rows, cols = asm.shape
    modes = strokes.shape[1]
    vmem = pl.BlockSpec(memory_space=VMEM)
    return pl.pallas_call(
        panel_kernel,
        out_shape=(VMEM((rows, cols), F32), VMEM((rows, modes), F32)),
        in_specs=[vmem] * 3,
        out_specs=(vmem, vmem),
        scratch_shapes=[
            VMEM((rows, modes), F32),
            VMEM((rows, 512), F32),
            VMEM((512, cols), F32),
            VMEM((512, 256), F32),
            VMEM((rows, 512), F32),
            VMEM((512, cols), F32),
            VMEM((512, cols), jnp.bfloat16),
            VMEM((512, cols), jnp.bfloat16),
            VMEM((512, modes), F32),
            VMEM((rows, modes), F32),
            VMEM((2, 4, rows // 8, modes), F32),
            VMEM((2, 3, rows // 32, modes), F32),
            DMA((4,)),
            DMA,
            DMA((4, P_CHUNKS)),
            DMA((4, P_CHUNKS)),
            DMA((2, Q_CHUNKS, 2)),
            DMA((2, Q_CHUNKS)),
            DMA((C_CHUNKS, 3)),
            DMA((C_CHUNKS,)),
            DMA((2, 3, 4)),
            DMA((2, 3, 4)),
            DMA((2, 3)),
            DMA((2, 3)),
            DMA((2, 3)),
            DMA((2, 3)),
            DMA((2, 3, 4)),
            DMA((2, 3, 4)),
        ],
        compiler_params=pltpu.CompilerParams(
            collective_id=1, has_side_effects=True, vmem_limit_bytes=32 << 20
        ),
        name="panels",
    )(resident(asm), inverses, resident(strokes))


def hand_out_kernel(factored, image, factored_out, image_out, sem):
    rows = factored.shape[0] // 4
    copies = [
        pltpu.make_async_copy(src.at[pl.ds(n * rows, rows)], dst.at[pl.ds(n * rows, rows)], sem.at[which, n])
        for which, (src, dst) in enumerate(((factored, factored_out), (image, image_out)))
        for n in range(4)
    ]
    for copy in copies:
        copy.start()
    for copy in copies:
        copy.wait()


def hand_out(factored, image):
    vmem = pl.BlockSpec(memory_space=VMEM)
    hbm = pl.BlockSpec(memory_space=pltpu.HBM)
    return pl.pallas_call(
        hand_out_kernel,
        out_shape=(pltpu.HBM(factored.shape, F32), pltpu.HBM(image.shape, F32)),
        in_specs=[vmem] * 2,
        out_specs=(hbm, hbm),
        scratch_shapes=[DMA((2, 4))],
        compiler_params=pltpu.CompilerParams(vmem_limit_bytes=8 << 20),
        name="hand_out",
    )(resident(factored), resident(image))


def on_device(far_field, inverses, test_table, trial_table, tile_list, tile_nodes, strokes):
    packed = make_pieces(tile_list, tile_nodes, test_table, trial_table, 16)
    arrived, far, held_strokes = exchange(packed, far_field, strokes)
    asm = place(arrived, far)
    return hand_out(*panels(asm, inverses, held_strokes))


def solution(mesh):
    return jax.shard_map(
        on_device,
        mesh=mesh,
        in_specs=(
            P("row", "col"),
            P(),
            P(("row", "col"), None),
            P(("row", "col"), None),
            P(("row", "col"), None),
            P(("row", "col"), None),
            P("col", None),
        ),
        out_specs=(P("row", "col"), P("row", None)),
        check_vma=False,
    )
```

```python
import jax
import jax.numpy as jnp
from jax import lax
from jax.experimental import pallas as pl
from jax.experimental.pallas import tpu as pltpu
from jax.sharding import PartitionSpec as P

MESH = pl.DeviceIdType.MESH
F32 = jnp.float32
VMEM = pltpu.VMEM
DMA = pltpu.SemaphoreType.DMA

LINK_TREE = (
    (0, 1, 2, 3), (1, 1, 1, 4), (3, 1, 1, 3), (3, 4, 3, 3),
    (0, 0, 4, 0), (1, 1, 0, 1), (3, 1, 0, 3), (0, 3, 0, 0),
    (0, 0, 2, 2), (0, 0, 2, 1), (0, 1, 2, 3), (0, 3, 2, 2),
    (4, 2, 2, 2), (2, 2, 2, 1), (2, 1, 1, 3), (2, 3, 3, 3),
)
TREE_DEPTH = (
    (0, 3, 4, 3, 1, 2, 3, 2, 2, 3, 4, 3, 3, 4, 5, 4),
    (0, 1, 2, 3, 3, 2, 3, 4, 4, 3, 4, 5, 3, 2, 3, 4),
    (0, 3, 4, 3, 3, 4, 5, 4, 2, 3, 4, 3, 1, 2, 3, 2),
    (0, 3, 2, 1, 3, 4, 3, 2, 4, 5, 4, 3, 3, 4, 3, 2),
)
STEPS_X = (1, 0, 3, 0)
STEPS_Y = (0, 1, 0, 3)


def table(values, index):
    found = jnp.int32(0)
    for at, value in enumerate(values):
        if value:
            found = found + jnp.where(index == at, jnp.int32(value), jnp.int32(0))
    return found


def mod4(value):
    return lax.rem(value, 4)


def split(a):
    high = a.astype(jnp.bfloat16)
    return high, (a - high.astype(F32)).astype(jnp.bfloat16)


def dot_split(a, b):
    def one(u, v):
        return jnp.dot(u, v, preferred_element_type=F32)

    return one(a[0], b[0]) + (one(a[0], b[1]) + one(a[1], b[0]))


def dot(a, b):
    return dot_split(split(a), split(b))


def pieces_kernel(
    tiles_hbm, nodes_hbm, test_hbm, trial_hbm, out_ref, test_ref, trial_ref, left, right, tiles_ref, nodes_ref,
    count, label, sem
):
    owned, quad = nodes_ref.shape
    dests = out_ref.shape[0]
    tile = test_ref.shape[1]
    block_cols = 8
    block_rows = 16
    loads = [
        pltpu.make_async_copy(src, dst, sem.at[n])
        for n, (src, dst) in enumerate(
            ((tiles_hbm, tiles_ref), (nodes_hbm, nodes_ref), (test_hbm, test_ref), (trial_hbm, trial_ref))
        )
    ]
    for load in loads:
        load.start()

    def clear(at, carry):
        count[at] = 0
        label[2 * at] = -1
        label[2 * at + 1] = -1
        return carry

    lax.fori_loop(0, dests, clear, 0)
    for load in loads:
        load.wait()
    sublane = lax.broadcasted_iota(jnp.int32, (8, tile), 0)

    def gather(t, slot):
        for q in range(0, quad, 8):
            nodes = [nodes_ref[t, q + k] for k in range(8)]
            for table_ref, to in ((test_ref, left), (trial_ref, right)):
                rows = [jnp.broadcast_to(table_ref[pl.ds(node, 1), :], (8, tile)) for node in nodes]
                for width in (1, 2, 4):
                    mask = lax.rem(sublane, 2 * width) < width
                    rows = [jnp.where(mask, rows[n], rows[n + 1]) for n in range(0, len(rows), 2)]
                to[slot, q : q + 8, :] = rows[0]

    def integrate(t, slot):
        piece = dot(left[slot].T, right[slot])
        block_row = lax.rem(tiles_ref[0, t], block_rows)
        block_col = tiles_ref[1, t]
        dest = lax.div(block_col, block_cols)
        place = count[dest]
        count[dest] = place + 1
        label[2 * dest + place] = block_row * block_cols + lax.rem(block_col, block_cols)
        out_ref[dest, pl.ds(pl.multiple_of(place * tile, tile), tile), :] = piece

    def two_tiles(n, carry):
        gather(2 * n + 1, 1)
        integrate(2 * n, 0)
        gather(2 * n + 2, 0)
        integrate(2 * n + 1, 1)
        return carry

    gather(0, 0)
    lax.fori_loop(0, owned // 2 - 1, two_tiles, 0)
    gather(owned - 1, 1)
    integrate(owned - 2, 0)
    integrate(owned - 1, 1)
    for d in range(dests):
        both = jnp.where(sublane == 0, label[2 * d], label[2 * d + 1])
        out_ref[d, 2 * tile : 2 * tile + 8, :] = both.astype(F32)


def make_pieces(tile_list, tile_nodes, test_table, trial_table, dests):
    tile = test_table.shape[1]
    quad = tile_nodes.shape[1]
    operands = (tile_list.T, tile_nodes, test_table, trial_table)
    return pl.pallas_call(
        pieces_kernel,
        out_shape=VMEM((dests, 2 * tile + 8, tile), F32),
        in_specs=[pl.BlockSpec(memory_space=pltpu.HBM)] * 4,
        out_specs=pl.BlockSpec(memory_space=VMEM),
        scratch_shapes=[
            VMEM(test_table.shape, F32),
            VMEM(trial_table.shape, F32),
            VMEM((2, quad, tile), F32),
            VMEM((2, quad, tile), F32),
            pltpu.SMEM(operands[0].shape, jnp.int32),
            pltpu.SMEM(tile_nodes.shape, jnp.int32),
            pltpu.SMEM((dests,), jnp.int32),
            pltpu.SMEM((2 * dests,), jnp.int32),
            DMA((4,)),
        ],
        compiler_params=pltpu.CompilerParams(vmem_limit_bytes=8 << 20),
        name="pieces",
    )(*(pltpu.with_memory_space_constraint(operand, pltpu.HBM) for operand in operands))


OFFSETS = sorted(
    ((dx, dy) for dx in range(4) for dy in range(4) if dx or dy),
    key=lambda o: min(o[0], 4 - o[0]) + min(o[1], 4 - o[1]),
)
FAR_PARTS = 8


def resident(array):
    return pltpu.with_memory_space_constraint(array, VMEM)


def exchange_kernel(packed, far_hbm, s_hbm, arrived, far, strokes, send_sem, recv_sem, own_sem, far_sem, s_sem):
    row = lax.axis_index("row")
    col = lax.axis_index("col")
    x, y = lax.div(col, 4), lax.rem(col, 4)
    peers = [mod4(x + dx) * 4 + mod4(y + dy) for dx, dy in OFFSETS]
    barrier = pltpu.get_barrier_semaphore()
    for peer in peers:
        pl.semaphore_signal(barrier, inc=1, device_id=(row, peer), device_id_type=MESH)
    size = far.shape[0] // FAR_PARTS
    load_s = pltpu.make_async_copy(s_hbm, strokes, s_sem)
    load_s.start()
    loads = []
    for j in range(FAR_PARTS):
        part = pl.ds(j * size, size)
        loads.append(pltpu.make_async_copy(far_hbm.at[part], far.at[part], far_sem.at[j]))
        loads[-1].start()
    pl.semaphore_wait(barrier, len(peers))
    copies = []
    for k, peer in enumerate(peers):
        copies.append(
            pltpu.make_async_remote_copy(
                src_ref=packed.at[peer],
                dst_ref=arrived.at[col],
                send_sem=send_sem.at[k],
                recv_sem=recv_sem.at[k],
                device_id=(row, peer),
                device_id_type=MESH,
            )
        )
        copies[-1].start()
    own = pltpu.make_async_copy(packed.at[col], arrived.at[col], own_sem)
    own.start()
    load_s.wait()
    for load in loads:
        load.wait()
    own.wait()
    for copy in copies:
        copy.wait()


def exchange(packed, far, strokes):
    n = len(OFFSETS)
    hbm = pl.BlockSpec(memory_space=pltpu.HBM)
    vmem = pl.BlockSpec(memory_space=VMEM)
    return pl.pallas_call(
        exchange_kernel,
        out_shape=(
            VMEM(packed.shape, F32),
            VMEM(far.shape, F32),
            VMEM(strokes.shape, F32),
        ),
        in_specs=[vmem, hbm, hbm],
        out_specs=(vmem,) * 3,
        scratch_shapes=[DMA((n,)), DMA((n,)), DMA, DMA((FAR_PARTS,)), DMA],
        compiler_params=pltpu.CompilerParams(
            collective_id=0, has_side_effects=True, vmem_limit_bytes=8 << 20
        ),
        name="exchange",
    )(
        resident(packed),
        pltpu.with_memory_space_constraint(far, pltpu.HBM),
        pltpu.with_memory_space_constraint(strokes, pltpu.HBM),
    )


def place_kernel(arrived, far, out, label):
    tile = arrived.shape[2]
    for d in range(arrived.shape[0]):
        for k in range(2):
            at = 2 * tile + k
            label[2 * d + k] = jnp.max(arrived[d, at : at + 1, :]).astype(jnp.int32)

    def add(s, carry):
        lab = label[s]

        @pl.when(lab >= 0)
        def _():
            rows = pl.ds(pl.multiple_of(lax.div(lab, 8) * tile, tile), tile)
            cols = pl.ds(pl.multiple_of(lax.rem(lab, 8) * tile, tile), tile)
            piece = arrived[lax.div(s, 2), pl.ds(pl.multiple_of(lax.rem(s, 2) * tile, tile), tile), :]
            out[rows, cols] = out[rows, cols] + piece

        return carry

    lax.fori_loop(0, label.shape[0], add, 0)


def place(arrived, far):
    vmem = pl.BlockSpec(memory_space=VMEM)
    return pl.pallas_call(
        place_kernel,
        out_shape=VMEM(far.shape, F32),
        in_specs=[vmem] * 2,
        out_specs=vmem,
        scratch_shapes=[pltpu.SMEM((2 * arrived.shape[0],), jnp.int32)],
        input_output_aliases={1: 0},
        compiler_params=pltpu.CompilerParams(vmem_limit_bytes=8 << 20),
        name="place",
    )(resident(arrived), resident(far))


P_CHUNKS = 16
P_ROWS = 128
Q_CHUNKS = 16
Q_ROWS = 32
C_CHUNKS = 4
LAG = 3
C_LAG = 2
G_STEP = 1


def panel_kernel(
    asm, inv_ref, s_ref, out_ref, img, g_ref, p_ref, q_ref, c_ref, l_ref, u_ref, u_high, u_low, us_ref,
    part, stage1, stage2, load_p, load_q, send_p, recv_p, send_q, recv_q, send_c, recv_c, send1, recv1, send2, recv2,
    send3, recv3, send4, recv4
):
    row = lax.axis_index("row")
    col = lax.axis_index("col")
    x, y = lax.div(col, 4), lax.rem(col, 4)
    z, core = lax.div(row, 2), lax.rem(row, 2)
    source = col == 0
    top = row == 0
    z_up = mod4(z + 1) * 2 + core
    z_down = mod4(z + 3) * 2 + core
    other = z * 2 + 1 - core
    neighbours = [mod4(x + STEPS_X[d]) * 4 + mod4(y + STEPS_Y[d]) for d in range(4)]
    link_tree = [table([LINK_TREE[v][d] for v in range(16)], col) for d in range(4)]
    depth = [table(TREE_DEPTH[t], col) for t in range(4)]

    across = [mod4(x + k) * 4 + y for k in range(4)]
    along = [x * 4 + mod4(y + k) for k in range(4)]
    barrier = pltpu.get_barrier_semaphore()
    for k in range(1, 4):
        pl.semaphore_signal(barrier, inc=1, device_id=(row, across[k]), device_id_type=MESH)
        pl.semaphore_signal(barrier, inc=1, device_id=(row, along[k]), device_id_type=MESH)
    for r in (z_up, z_down, other):
        pl.semaphore_signal(barrier, inc=1, device_id=(r, col), device_id_type=MESH)

    quarter = p_ref.shape[0] // 4

    def load_quarter(k):
        rows = pl.ds(pl.multiple_of(k * quarter, quarter), quarter)
        return pltpu.make_async_copy(asm.at[rows, pl.ds(0, 512)], p_ref.at[rows, :], load_p.at[k])

    load_rows = pltpu.make_async_copy(asm.at[pl.ds(0, 512), :], q_ref, load_q)

    @pl.when(source)
    def _():
        for k in range(4):
            load_quarter(k).start()

    @pl.when(top)
    def _():
        load_rows.start()

    pl.semaphore_wait(barrier, 9)

    @pl.when(top)
    def _():
        load_rows.wait()

    def p_copy(t, i, d):
        at = p_ref.at[
            pl.ds(pl.multiple_of(i * P_ROWS, P_ROWS), P_ROWS), pl.ds(t * 128, 128)
        ]
        return pltpu.make_async_remote_copy(
            src_ref=at,
            dst_ref=at,
            send_sem=send_p.at[d, i],
            recv_sem=recv_p.at[t, i],
            device_id=(row, neighbours[d]),
            device_id_type=MESH,
        )

    def q_copy(h, j, way, r):
        at = q_ref.at[pl.ds(pl.multiple_of(j * Q_ROWS, Q_ROWS), Q_ROWS), pl.ds(h * 512, 512)]
        return pltpu.make_async_remote_copy(
            src_ref=at,
            dst_ref=at,
            send_sem=send_q.at[h, j, way],
            recv_sem=recv_q.at[h, j],
            device_id=(r, col),
            device_id_type=MESH,
        )

    def c_copy(i, way, r, first):
        rows = pl.ds(pl.multiple_of(i * P_ROWS, P_ROWS), P_ROWS)
        here = c_ref.at[rows, :]
        start = pl.multiple_of(jnp.where(i < C_CHUNKS // 2, 256, 0), 256)
        return pltpu.make_async_remote_copy(
            src_ref=p_ref.at[rows, pl.ds(start, 256)] if first else here,
            dst_ref=here,
            send_sem=send_c.at[i, way],
            recv_sem=recv_c.at[i],
            device_id=(r, col),
            device_id_type=MESH,
        )

    lead = core == 0
    q_depth = [z + core, mod4(4 - z) + core]
    q_next = [(z_up, lead & (z < 3)), (z_down, lead & (z != 1))]
    deepest = jnp.maximum(jnp.maximum(depth[0], depth[1]), jnp.maximum(depth[2], depth[3]))
    c_depth = 1 + LAG * deepest + C_LAG * (jnp.where(z == 2, 2, jnp.where(z == 0, 0, 1)) + core)
    big = out_ref.shape[0] // 8

    def step(s, carry):
        for t in range(4):
            i = s - LAG * depth[t]

            @pl.when((i >= 0) & (i < P_CHUNKS))
            def _(t=t, i=i):
                if t == 0:

                    @pl.when(source & (lax.rem(i, P_CHUNKS // 4) == 0))
                    def _():
                        load_quarter(lax.div(i, P_CHUNKS // 4)).wait()

                @pl.when(jnp.logical_not(source))
                def _():
                    p_copy(t, i, 0).wait_recv()

                for d in range(4):

                    @pl.when(link_tree[d] == t)
                    def _(d=d):
                        p_copy(t, i, d).start()

        for h in range(2):
            j = s - LAG * q_depth[h]

            @pl.when((j >= 0) & (j < Q_CHUNKS))
            def _(h=h, j=j):
                @pl.when(jnp.logical_not(top))
                def _():
                    q_copy(h, j, 0, other).wait_recv()

                @pl.when(lead)
                def _():
                    q_copy(h, j, 0, other).start()

                @pl.when(q_next[h][1])
                def _():
                    q_copy(h, j, 1, q_next[h][0]).start()

        i = s - c_depth

        @pl.when((i >= 0) & (i < C_CHUNKS))
        def _():
            @pl.when(top)
            def _():
                c_copy(i, 0, other, True).start()
                c_copy(i, 1, z_up, True).start()
                c_copy(i, 2, z_down, True).start()

            @pl.when(jnp.logical_not(top))
            def _():
                c_copy(i, 0, other, False).wait_recv()

                @pl.when(lead)
                def _():
                    c_copy(i, 0, other, False).start()

                @pl.when(lead & (z == 1))
                def _():
                    c_copy(i, 1, z_up, False).start()

        n = s - G_STEP

        @pl.when((n >= 0) & (n < 8))
        def _():
            mine = pl.ds(pl.multiple_of(n * big, big), big)
            g_ref[mine, :] = dot(asm[mine, :], s_ref[...])

        return carry

    lax.fori_loop(0, max(P_CHUNKS + 5 * LAG, C_CHUNKS + 1 + 5 * LAG + 3 * C_LAG), step, 0)

    @pl.when(top)
    def _():
        c_ref[0:256, :] = p_ref[0:256, 256:512]
        c_ref[256:512, :] = p_ref[256:512, 0:256]

    inv0, inv1 = split(inv_ref[0]), split(inv_ref[1])
    upper0 = q_ref[0:256, :]
    ratio = dot_split(split(c_ref[256:512, :]), inv0)
    u_ref[0:256, :] = upper0
    u_ref[256:512, :] = q_ref[256:512, :] - dot(ratio, upper0)

    @pl.when(source)
    def _():
        u_ref[0:256, 0:256] = jnp.zeros((256, 256), F32)
        u_ref[256:512, 0:512] = jnp.zeros((256, 512), F32)

    u_high[...], u_low[...] = split(u_ref[...])
    us_ref[...] = dot_split((u_high[...], u_low[...]), split(s_ref[...]))

    rows = part.shape[0]
    half = rows // 2
    small = big // 4
    outer = (x, y)
    inner = (y, x)
    outer_peers = (across, along)
    inner_peers = (along, across)

    def at(start, count):
        return pl.ds(pl.multiple_of(start, count), count)

    def remote(src, dst, send, recv, peer):
        return pltpu.make_async_remote_copy(
            src_ref=src, dst_ref=dst, send_sem=send, recv_sem=recv, device_id=(row, peer), device_id_type=MESH
        )

    def piece(h, m):
        return at(mod4(inner[h] + m) * small, small)

    def second_copy(h, m):
        return remote(
            stage1.at[h, 3, piece(h, m), :],
            stage2.at[h, m - 1],
            send2.at[h, m - 1],
            recv2.at[h, m - 1],
            inner_peers[h][m],
        )

    def third_copy(h, m):
        here = img.at[at(h * half + outer[h] * big + inner[h] * small, small), :]
        return remote(here, here, send3.at[h, m - 1], recv3.at[h, m - 1], inner_peers[h][m])

    def fourth_copy(h, k, m):
        here = img.at[at(h * half + outer[h] * big + mod4(inner[h] + 4 - m) * small, small), :]
        return remote(here, here, send4.at[h, k - 1, m], recv4.at[h, k - 1, m], outer_peers[h][k])

    def finish_tile(j, carry):
        mine = at(j * big, big)
        lower = l_ref[mine, :]
        out_ref[mine, :] = asm[mine, :] - dot_split(split(lower), (u_high[...], u_low[...]))

        @pl.when(source & ((row > 0) | (j > 0)))
        def _():
            out_ref[mine, 0:256] = l_ref[mine, 0:256]

        @pl.when(source & ((row > 0) | (j > 1)))
        def _():
            out_ref[mine, 256:512] = l_ref[mine, 256:512]

        return carry

    order = (2, 1, 3)
    pieces = (2, 1, 3, 0)

    def first_copy(h, k, m):
        to = mod4(outer[h] + k)
        return remote(
            part.at[at(h * half + to * big + mod4(inner[h] + m) * small, small), :],
            stage1.at[h, k - 1, piece(h, m), :],
            send1.at[h, k - 1, m],
            recv1.at[h, k - 1, m],
            to * 4 + y if h == 0 else x * 4 + to,
        )

    def two_tiles(n, carry):
        k = table((2, 1, 3, 0), n)
        tiles = []
        for h in range(2):
            j = h * 4 + mod4(outer[h] + k)
            tiles.append((at(j * big, big), (row > 0) | (j > 0), (row > 0) | (j > 1)))
        lower0 = [jnp.where(b0, dot_split(split(p_ref[m, 0:256]), inv0), 0.0) for m, b0, _ in tiles]
        beside = split(c_ref[0:256, :])
        rest = [p_ref[m, 256:512] - dot_split(split(low), beside) for (m, _, _), low in zip(tiles, lower0)]
        lower1 = [jnp.where(b1, dot_split(split(r), inv1), 0.0) for (_, _, b1), r in zip(tiles, rest)]
        us0, us1 = split(us_ref[0:256, :]), split(us_ref[256:512, :])
        for (m, _, _), low0, low1 in zip(tiles, lower0, lower1):
            l_ref[m, 0:256] = low0
            l_ref[m, 256:512] = low1
            part[m, :] = g_ref[m, :] - (dot_split(split(low0), us0) + dot_split(split(low1), us1))

        @pl.when(source)
        def _():
            for m, b0, b1 in tiles:
                low0, low1 = l_ref[m, 0:256], l_ref[m, 256:512]
                left = p_ref[m, 256:512] - dot(low0, c_ref[0:256, :])
                change0 = jnp.where(b0, low0 - p_ref[m, 0:256], 0.0)
                change1 = jnp.where(b1, low1 - left, 0.0)
                part[m, :] += dot(change0, s_ref[0:256, :]) + dot(change1, s_ref[256:512, :])

        @pl.when(k > 0)
        def _():
            for m in pieces:
                for h in range(2):
                    first_copy(h, k, m).start()

        return carry

    lax.fori_loop(0, 4, two_tiles, 0)

    for m in pieces:
        for h in range(2):
            for k in order:
                first_copy(h, k, m).wait_recv()
            total = part[at(h * half + outer[h] * big + mod4(inner[h] + m) * small, small), :]
            for k in range(1, 4):
                total = total + stage1[h, k - 1, piece(h, m), :]
            stage1[h, 3, piece(h, m), :] = total
            if m:
                second_copy(h, m).start()
    lax.fori_loop(0, 2, finish_tile, 0)
    for h in range(2):
        for m in order:
            second_copy(h, m).wait_recv()
        total = stage1[h, 3, piece(h, 0), :]
        for m in range(1, 4):
            total = total + stage2[h, m - 1]
        img[at(h * half + outer[h] * big + inner[h] * small, small), :] = total
        for m in order:
            third_copy(h, m).start()
        for k in order:
            fourth_copy(h, k, 0).start()
    lax.fori_loop(2, 4, finish_tile, 0)
    for m in (1, 3, 2):
        for h in range(2):
            third_copy(h, m).wait_recv()
            for k in order:
                fourth_copy(h, k, m).start()
    lax.fori_loop(4, 8, finish_tile, 0)
    for h in range(2):
        for k in order:
            for m in range(4):
                fourth_copy(h, k, m).wait_recv()
    for h in range(2):
        for k in order:
            second_copy(h, k).wait_send()
            third_copy(h, k).wait_send()
            for m in range(4):
                first_copy(h, k, m).wait_send()
                fourth_copy(h, k, m).wait_send()

    def drain_p(i, carry):
        for d in range(4):

            @pl.when(link_tree[d] < 4)
            def _(d=d):
                p_copy(0, i, d).wait_send()

        return carry

    lax.fori_loop(0, P_CHUNKS, drain_p, 0)

    def drain_q(j, carry):
        for h in range(2):

            @pl.when(lead)
            def _(h=h):
                q_copy(h, j, 0, other).wait_send()

            @pl.when(q_next[h][1])
            def _(h=h):
                q_copy(h, j, 1, q_next[h][0]).wait_send()

        return carry

    lax.fori_loop(0, Q_CHUNKS, drain_q, 0)

    def drain_c(i, carry):
        @pl.when(lead)
        def _():
            c_copy(i, 0, other, False).wait_send()

        @pl.when(top | (lead & (z == 1)))
        def _():
            c_copy(i, 1, z_up, False).wait_send()

        @pl.when(top)
        def _():
            c_copy(i, 2, z_down, False).wait_send()

        return carry

    lax.fori_loop(0, C_CHUNKS, drain_c, 0)


def panels(asm, inverses, strokes):
    rows, cols = asm.shape
    modes = strokes.shape[1]
    vmem = pl.BlockSpec(memory_space=VMEM)
    return pl.pallas_call(
        panel_kernel,
        out_shape=(VMEM((rows, cols), F32), VMEM((rows, modes), F32)),
        in_specs=[vmem] * 3,
        out_specs=(vmem, vmem),
        scratch_shapes=[
            VMEM((rows, modes), F32),
            VMEM((rows, 512), F32),
            VMEM((512, cols), F32),
            VMEM((512, 256), F32),
            VMEM((rows, 512), F32),
            VMEM((512, cols), F32),
            VMEM((512, cols), jnp.bfloat16),
            VMEM((512, cols), jnp.bfloat16),
            VMEM((512, modes), F32),
            VMEM((rows, modes), F32),
            VMEM((2, 4, rows // 8, modes), F32),
            VMEM((2, 3, rows // 32, modes), F32),
            DMA((4,)),
            DMA,
            DMA((4, P_CHUNKS)),
            DMA((4, P_CHUNKS)),
            DMA((2, Q_CHUNKS, 2)),
            DMA((2, Q_CHUNKS)),
            DMA((C_CHUNKS, 3)),
            DMA((C_CHUNKS,)),
            DMA((2, 3, 4)),
            DMA((2, 3, 4)),
            DMA((2, 3)),
            DMA((2, 3)),
            DMA((2, 3)),
            DMA((2, 3)),
            DMA((2, 3, 4)),
            DMA((2, 3, 4)),
        ],
        compiler_params=pltpu.CompilerParams(
            collective_id=1, has_side_effects=True, vmem_limit_bytes=32 << 20
        ),
        name="panels",
    )(resident(asm), inverses, resident(strokes))


def hand_out_kernel(factored, image, factored_out, image_out, sem):
    rows = factored.shape[0] // 4
    copies = [
        pltpu.make_async_copy(src.at[pl.ds(n * rows, rows)], dst.at[pl.ds(n * rows, rows)], sem.at[which, n])
        for which, (src, dst) in enumerate(((factored, factored_out), (image, image_out)))
        for n in range(4)
    ]
    for copy in copies:
        copy.start()
    for copy in copies:
        copy.wait()


def hand_out(factored, image):
    vmem = pl.BlockSpec(memory_space=VMEM)
    hbm = pl.BlockSpec(memory_space=pltpu.HBM)
    return pl.pallas_call(
        hand_out_kernel,
        out_shape=(pltpu.HBM(factored.shape, F32), pltpu.HBM(image.shape, F32)),
        in_specs=[vmem] * 2,
        out_specs=(hbm, hbm),
        scratch_shapes=[DMA((2, 4))],
        compiler_params=pltpu.CompilerParams(vmem_limit_bytes=8 << 20),
        name="hand_out",
    )(resident(factored), resident(image))


def on_device(far_field, inverses, test_table, trial_table, tile_list, tile_nodes, strokes):
    packed = make_pieces(tile_list, tile_nodes, test_table, trial_table, 16)
    arrived, far, held_strokes = exchange(packed, far_field, strokes)
    asm = place(arrived, far)
    return hand_out(*panels(asm, inverses, held_strokes))


def solution(mesh):
    return jax.shard_map(
        on_device,
        mesh=mesh,
        in_specs=(
            P("row", "col"),
            P(),
            P(("row", "col"), None),
            P(("row", "col"), None),
            P(("row", "col"), None),
            P(("row", "col"), None),
            P("col", None),
        ),
        out_specs=(P("row", "col"), P("row", None)),
        check_vma=False,
    )
```
